32 devices in a mesh: tensor: 4 (over y, x), context: 2 (over core), dp: 4 (over z).
Axes of the slice: x: 2, y: 2, z: 4, core: 2. Of those that a mesh axis runs over, the one named last changes fastest.
Arguments:
- inputs: bfloat16 [4, 512, 1024], P('dp', 'context'), may hold values from -6 to 6
- norm_gain1: float32 [1024], replicated, may hold values from 0.5 to 1.5
- w_query: bfloat16 [1024, 512], P(None, 'tensor'), may hold values from -0.1875 to 0.1875
- w_key: bfloat16 [1024, 512], P(None, 'tensor'), may hold values from -0.1875 to 0.1875
- w_value: bfloat16 [1024, 1024], P(None, 'tensor'), may hold values from -0.1875 to 0.1875
- w_gate_out: bfloat16 [1024, 1024], P(None, 'tensor'), may hold values from -0.1875 to 0.1875
- w_low_down: bfloat16 [1024, 16], replicated, may hold values from -0.1875 to 0.1875
- w_low_up: bfloat16 [16, 512], P(None, 'tensor'), may hold values from -3 to 3
- forget_bias: float32 [512], P('tensor'), may hold values from -1 to 9, as said below
- head_gain: float32 [256], replicated, may hold values from 0.5 to 1.5
- w_output: bfloat16 [1024, 1024], P('tensor'), may hold values from -0.1875 to 0.1875
- norm_gain2: float32 [1024], replicated, may hold values from 0.5 to 1.5
- w_ffn_gate: bfloat16 [1024, 2816], P(None, 'tensor'), may hold values from -0.1875 to 0.1875
- w_ffn_up: bfloat16 [1024, 2816], P(None, 'tensor'), may hold values from -0.1875 to 0.1875
- w_ffn_down: bfloat16 [2816, 1024], P('tensor'), may hold values from -0.109375 to 0.109375
- cotangent: bfloat16 [4, 512, 1024], P('dp', 'context'), may hold values from -6 to 6
Outputs:
- result: bfloat16 [4, 512, 1024], P('dp', 'context')
- grad_inputs: float32 [4, 512, 1024], P('dp', 'context')
- grad_gain1: float32 [1024], P(('context', 'dp'))
- grad_w_query: float32 [1024, 512], P(('context', 'dp'), 'tensor')
- grad_w_key: float32 [1024, 512], P(('context', 'dp'), 'tensor')
- grad_w_value: float32 [1024, 1024], P(('context', 'dp'), 'tensor')
- grad_w_gate_out: float32 [1024, 1024], P(('context', 'dp'), 'tensor')
- grad_w_low_down: float32 [1024, 16], P(('context', 'dp'))
- grad_w_low_up: float32 [16, 512], P(None, ('tensor', 'context', 'dp'))
- grad_forget_bias: float32 [512], P(('tensor', 'context', 'dp'))
- grad_head_gain: float32 [256], P(('context', 'dp'))
- grad_w_output: float32 [1024, 1024], P('tensor', ('context', 'dp'))
- grad_gain2: float32 [1024], P(('context', 'dp'))
- grad_w_ffn_gate: float32 [1024, 2816], P(('context', 'dp'), 'tensor')
- grad_w_ffn_up: float32 [1024, 2816], P(('context', 'dp'), 'tensor')
- grad_w_ffn_down: float32 [2816, 1024], P('tensor', ('context', 'dp'))
The draws below stay inside these ranges and needn't reach their ends.
Inputs may be any that keep to these rules, and one draw needn't show every extreme that they name: `forget_bias`: bias of the forget gate's logits, one per key channel.
All inputs are finite; a program needn't handle non-finite values.
Results may differ from the reference program's by a relative error of at most 0.012.
The reference program's roundings to bfloat16 on the way (of `normed_one`, `gated`, `normed_two`, `mixed_act` and `grad_attn`) count: a program that leaves them out, or rounds other values in their place, can miss the bound.
Values sent between devices are 32-bit elements; how exact they have to be, the bound alone decides.
A program may use at most 128 MiB of HBM per device.

```python
import jax
import jax.numpy as jnp
from jax import lax

D = 1024
HEADS = 4
KEY = 128
VAL = 256
FF = 2816
RANK = 16
BLOCK = 64
SEQS = 4
LEN = 512
KEY_ALL = 512
VAL_ALL = 1024


def draw_forget_bias(key, part):
    return jax.random.uniform(key, (KEY_ALL,), jnp.float32, -1.0, 8.0)


def block_levels(own_key, dims, pieces, least, top_value):
    loudness = 1.0
    for dim, parts in pieces:
        heights = jax.random.uniform(jax.random.fold_in(jax.random.fold_in(own_key, 6), dim), (parts,), jnp.float32, least / len(pieces), top_value / len(pieces))
        loudness = loudness * jnp.repeat(jnp.exp(heights), dims[dim] // parts).reshape((-1,) + (1,) * (len(dims) - 1 - dim))
    return loudness


def normal_values(rng, extent, scale, limit, cuts=(), kind=jnp.bfloat16):
    array = scale * jax.random.normal(rng, extent, jnp.float32)
    if cuts:
        array = array * block_levels(rng, extent, cuts, -0.22, 0.18)
    return jnp.clip(array, -limit, limit).astype(kind)


def setup_inputs(seed: int = 0) -> dict:
    key_of = jax.random.split(jax.random.key(seed), 17)
    return {
        "inputs": normal_values(key_of[0], (SEQS, LEN, D), 1.0, 6.0, ((0, 4), (1, 2))),
        "norm_gain1": jnp.clip(1.0 + 0.1 * jax.random.normal(key_of[1], (D,), jnp.float32), 0.5, 1.5),
        "w_query": normal_values(key_of[2], (D, KEY_ALL), D ** -0.5, 0.1875, ((1, 4),)),
        "w_key": normal_values(key_of[3], (D, KEY_ALL), D ** -0.5, 0.1875, ((1, 4),)),
        "w_value": normal_values(key_of[4], (D, VAL_ALL), D ** -0.5, 0.1875, ((1, 4),)),
        "w_gate_out": normal_values(key_of[5], (D, VAL_ALL), D ** -0.5, 0.1875, ((1, 4),)),
        "w_low_down": normal_values(key_of[6], (D, RANK), D ** -0.5, 0.1875),
        "w_low_up": normal_values(key_of[7], (RANK, KEY_ALL), (RANK // 4) ** -0.5, 3.0, ((1, 4),)),
        "forget_bias": draw_forget_bias(jax.random.fold_in(key_of[16], 71), 0),
        "head_gain": jnp.clip(1.0 + 0.1 * jax.random.normal(key_of[9], (VAL,), jnp.float32), 0.5, 1.5),
        "w_output": normal_values(key_of[10], (VAL_ALL, D), VAL_ALL ** -0.5, 0.1875, ((0, 4),)),
        "norm_gain2": jnp.clip(1.0 + 0.1 * jax.random.normal(key_of[11], (D,), jnp.float32), 0.5, 1.5),
        "w_ffn_gate": normal_values(key_of[12], (D, FF), D ** -0.5, 0.1875, ((1, 4),)),
        "w_ffn_up": normal_values(key_of[13], (D, FF), D ** -0.5, 0.1875, ((1, 4),)),
        "w_ffn_down": normal_values(key_of[14], (FF, D), FF ** -0.5, 0.109375, ((0, 4),)),
        "cotangent": normal_values(key_of[15], (SEQS, LEN, D), 1.0, 6.0, ((0, 4), (1, 2))),
    }


EPS_MODEL = 1e-06
EPS_HEAD = 1e-05
GATE_NORM = 16.0
HIGHEST = lax.Precision.HIGHEST

def block_step(carried, block_in):
    queries, keys_in, values_in, log_rates = block_in
    cumul_log = jnp.cumsum(log_rates, axis=0)
    anchor = 0.5 * cumul_log[-1]
    scores = jnp.dot(queries * jnp.exp(cumul_log - anchor), (keys_in * jnp.exp(anchor - cumul_log)).T, precision=HIGHEST)
    length = queries.shape[0]
    causal = jnp.arange(length)[:, None] >= jnp.arange(length)[None, :]
    scores = jnp.where(causal, scores, 0.0)
    outputs = jnp.dot(scores, values_in, precision=HIGHEST) + jnp.dot(queries * jnp.exp(cumul_log), carried, precision=HIGHEST)
    end_log = cumul_log[-1]
    updated = jnp.exp(end_log)[:, None] * carried + jnp.dot((keys_in * jnp.exp(end_log - cumul_log)).T, values_in, precision=HIGHEST)
    return (updated, outputs)

def gla_core(queries, keys_in, values_in, log_rates, initial):
    block_count = queries.shape[0] // BLOCK
    blocks = (queries.reshape(block_count, BLOCK, -1), keys_in.reshape(block_count, BLOCK, -1), values_in.reshape(block_count, BLOCK, -1), log_rates.reshape(block_count, BLOCK, -1))
    final_state, outputs = lax.scan(block_step, initial, blocks)
    return (outputs.reshape(queries.shape[0], -1), final_state)

def rms_scale(rows_in):
    return lax.rsqrt(lax.optimization_barrier(jnp.mean(rows_in * rows_in, axis=-1, keepdims=True)) + EPS_MODEL)

def norm_back(rows_in, scale_rows, gain_in, grad_normed):
    weighted = gain_in * grad_normed
    grad_gain = lax.optimization_barrier(jnp.sum(grad_normed * rows_in * scale_rows, axis=0))
    grad_rows = scale_rows * (weighted - rows_in * scale_rows * scale_rows * lax.optimization_barrier(jnp.mean(weighted * rows_in, axis=-1, keepdims=True)))
    return (grad_rows, grad_gain)

def head_gate(outputs, head_gain, gate_in):
    scale_rows = lax.rsqrt(lax.optimization_barrier(jnp.mean(outputs * outputs, axis=-1, keepdims=True)) + EPS_HEAD)
    return outputs * scale_rows * head_gain * jax.nn.silu(gate_in)

def silu_grad(values_in):
    sigmoid_v = jax.nn.sigmoid(values_in)
    return sigmoid_v * (1.0 + values_in * (1.0 - sigmoid_v))

def reference(inputs, norm_gain1, w_query, w_key, w_value, w_gate_out, w_low_down, w_low_up, forget_bias, head_gain, w_output, norm_gain2, w_ffn_gate, w_ffn_up, w_ffn_down, cotangent):
    key_scale = KEY ** (-0.5)
    core_heads = jax.vmap(gla_core)
    bf16 = jnp.bfloat16
    f32 = jnp.float32

    def to_heads(packed, width_head):
        return packed.reshape(LEN, HEADS, width_head).transpose(1, 0, 2)

    def from_heads(packed):
        return packed.transpose(1, 0, 2).reshape(LEN, -1)

    def one_sequence(totals, seq_pair):
        seq_in, seq_cot = seq_pair
        rows_in = seq_in.astype(f32)
        scale_one = rms_scale(rows_in)
        normed_one = (rows_in * scale_one * norm_gain1).astype(bf16)
        queries = jnp.dot(normed_one, w_query, preferred_element_type=f32) * key_scale
        keys_proj = jnp.dot(normed_one, w_key, preferred_element_type=f32)
        values_proj = jnp.dot(normed_one, w_value, preferred_element_type=f32)
        gate_in = jnp.dot(normed_one, w_gate_out, preferred_element_type=f32)
        low_rank = jnp.dot(normed_one, w_low_down, preferred_element_type=f32)
        logits = jnp.dot(low_rank, w_low_up.astype(f32), precision=HIGHEST) + forget_bias
        log_rates = jax.nn.log_sigmoid(logits) / GATE_NORM
        initial = jnp.zeros((HEADS, KEY, VAL), f32)
        core_out, core_pull = jax.vjp(core_heads, to_heads(queries, KEY), to_heads(keys_proj, KEY), to_heads(values_proj, VAL), to_heads(log_rates, KEY), initial)
        outputs = core_out[0].transpose(1, 0, 2)
        gate_heads = gate_in.reshape(LEN, HEADS, VAL)
        gated, gate_pull = jax.vjp(head_gate, outputs, head_gain, gate_heads)
        gated_bf = gated.reshape(LEN, VAL_ALL).astype(bf16)
        hidden_res = rows_in + jnp.dot(gated_bf, w_output, preferred_element_type=f32)
        scale_two = rms_scale(hidden_res)
        normed_two = (hidden_res * scale_two * norm_gain2).astype(bf16)
        ffn_gate = jnp.dot(normed_two, w_ffn_gate, preferred_element_type=f32)
        ffn_up = jnp.dot(normed_two, w_ffn_up, preferred_element_type=f32)
        mixed_act = (jax.nn.silu(ffn_gate) * ffn_up).astype(bf16)
        result = hidden_res + jnp.dot(mixed_act, w_ffn_down, preferred_element_type=f32)
        grad_res = seq_cot.astype(f32)
        grad_down = jnp.dot(mixed_act.T, seq_cot, preferred_element_type=f32)
        grad_mixed = jnp.dot(seq_cot, w_ffn_down.T, preferred_element_type=f32)
        grad_gate = (grad_mixed * ffn_up * silu_grad(ffn_gate)).astype(bf16)
        grad_up = (grad_mixed * jax.nn.silu(ffn_gate)).astype(bf16)
        grad_ffn_gate = jnp.dot(normed_two.T, grad_gate, preferred_element_type=f32)
        grad_ffn_up = jnp.dot(normed_two.T, grad_up, preferred_element_type=f32)
        grad_normed_two = jnp.dot(grad_gate, w_ffn_gate.T, preferred_element_type=f32) + jnp.dot(grad_up, w_ffn_up.T, preferred_element_type=f32)
        grad_two_rows, grad_gain_two = norm_back(hidden_res, scale_two, norm_gain2, grad_normed_two)
        grad_hidden = grad_res + grad_two_rows
        grad_attn = grad_hidden.astype(bf16)
        grad_out_proj = jnp.dot(gated_bf.T, grad_attn, preferred_element_type=f32)
        grad_gated = jnp.dot(grad_attn, w_output.T, preferred_element_type=f32).reshape(LEN, HEADS, VAL)
        grad_outputs, grad_gain_head, grad_gate_heads = gate_pull(grad_gated)
        grad_q_h, grad_k_h, grad_v_h, grad_lr_h, unused_state = core_pull((grad_outputs.transpose(1, 0, 2), jnp.zeros_like(core_out[1])))
        grad_logits = from_heads(grad_lr_h) * jax.nn.sigmoid(-logits) / GATE_NORM
        grad_bias = lax.optimization_barrier(jnp.sum(grad_logits, axis=0))
        grad_low_up = jnp.dot(low_rank.T, grad_logits, precision=HIGHEST)
        grad_low = jnp.dot(grad_logits, w_low_up.astype(f32).T, precision=HIGHEST)
        grad_low_down = jnp.dot(normed_one.astype(f32).T, grad_low, precision=HIGHEST)
        grad_q = (from_heads(grad_q_h) * key_scale).astype(bf16)
        grad_k = from_heads(grad_k_h).astype(bf16)
        grad_v = from_heads(grad_v_h).astype(bf16)
        grad_g = grad_gate_heads.reshape(LEN, VAL_ALL).astype(bf16)
        grad_query_w = jnp.dot(normed_one.T, grad_q, preferred_element_type=f32)
        grad_key_w = jnp.dot(normed_one.T, grad_k, preferred_element_type=f32)
        grad_value_w = jnp.dot(normed_one.T, grad_v, preferred_element_type=f32)
        grad_gate_w = jnp.dot(normed_one.T, grad_g, preferred_element_type=f32)
        grad_normed_one = jnp.dot(grad_q, w_query.T, preferred_element_type=f32) + jnp.dot(grad_k, w_key.T, preferred_element_type=f32) + jnp.dot(grad_v, w_value.T, preferred_element_type=f32) + jnp.dot(grad_g, w_gate_out.T, preferred_element_type=f32) + jnp.dot(grad_low, w_low_down.astype(f32).T, precision=HIGHEST)
        grad_one_rows, grad_gain_one = norm_back(rows_in, scale_one, norm_gain1, grad_normed_one)
        grad_in = grad_hidden + grad_one_rows
        new_terms = (grad_gain_one, grad_query_w, grad_key_w, grad_value_w, grad_gate_w, grad_low_down, grad_low_up, grad_bias, grad_gain_head, grad_out_proj, grad_gain_two, grad_ffn_gate, grad_ffn_up, grad_down)
        new_totals = tuple((old + new for old, new in zip(totals, new_terms)))
        return (new_totals, (result.astype(bf16), grad_in))
    start_totals = tuple((jnp.zeros(shaped.shape, f32) for shaped in (norm_gain1, w_query, w_key, w_value, w_gate_out, w_low_down, w_low_up, forget_bias, head_gain, w_output, norm_gain2, w_ffn_gate, w_ffn_up, w_ffn_down)))
    totals, (results, grads_in) = lax.scan(one_sequence, start_totals, (inputs, cotangent))
    grad_gain1, grad_w_query, grad_w_key, grad_w_value, grad_w_gate_out, grad_w_low_down, grad_w_low_up, grad_forget_bias, grad_head_gain, grad_w_output, grad_gain2, grad_w_ffn_gate, grad_w_ffn_up, grad_w_ffn_down = totals
    return (results, grads_in, grad_gain1, grad_w_query, grad_w_key, grad_w_value, grad_w_gate_out, grad_w_low_down, grad_w_low_up, grad_forget_bias, grad_head_gain, grad_w_output, grad_gain2, grad_w_ffn_gate, grad_w_ffn_up, grad_w_ffn_down)
```

```python
import functools

import jax
import jax.numpy as jnp
from jax import lax
from jax.experimental import pallas as pl
from jax.experimental.pallas import tpu as pltpu
from jax.sharding import PartitionSpec as P

BLOCK = 64


EPS_MODEL = 1e-06
EPS_HEAD = 1e-05
GATE_NORM = 16.0
HIGHEST = lax.Precision.HIGHEST


VMEM_LIMIT = 62 * 1024 * 1024
VMEM = pltpu.MemorySpace.VMEM
MESH_ID = pl.DeviceIdType.MESH


def hdot(left, right, dims):
    return lax.dot_general(
        left, right, (dims, ((), ())), precision=HIGHEST, preferred_element_type=jnp.float32
    )


def mm(left, right):
    return jnp.dot(left, right, preferred_element_type=jnp.float32)


def mm_nt(left, right):
    return lax.dot_general(
        left, right, (((1,), (1,)), ((), ())), preferred_element_type=jnp.float32
    )


def column_of(row, height):
    return jnp.broadcast_to(row, (height, row.shape[1])).T


def triangle(length):
    rows = lax.broadcasted_iota(jnp.int32, (length, length), 0)
    cols = lax.broadcasted_iota(jnp.int32, (length, length), 1)
    return rows >= cols


def rms_scale(rows_in):
    return lax.rsqrt(jnp.mean(rows_in * rows_in, axis=-1, keepdims=True) + EPS_MODEL)


def norm_back(rows_in, scale_rows, gain_in, grad_normed):
    weighted = gain_in * grad_normed
    grad_gain = jnp.sum(grad_normed * rows_in * scale_rows, axis=0, keepdims=True)
    grad_rows = scale_rows * (
        weighted
        - rows_in * scale_rows * scale_rows * jnp.mean(weighted * rows_in, axis=-1, keepdims=True)
    )
    return (grad_rows, grad_gain)


def gla_states(proj, rates, cumuls_ref, states_ref, pair_ref):
    tokens, key_dim = rates.shape
    value_dim = states_ref.shape[2]
    ones_low = triangle(BLOCK).astype(jnp.float32)
    state = jnp.zeros((key_dim, value_dim), jnp.float32)
    before = jnp.zeros((1, key_dim), jnp.float32)
    for block in range(tokens // BLOCK):
        span = pl.ds(block * BLOCK, BLOCK)
        keys_in = proj[span, key_dim : 2 * key_dim]
        values_in = proj[span, 2 * key_dim : 2 * key_dim + value_dim]
        cumul = hdot(ones_low, rates[span, :], ((1,), (0,)))
        cumuls_ref[span, :] = cumul
        end_log = cumul[BLOCK - 1 :, :]
        states_ref[block] = state
        added = hdot(keys_in * jnp.exp(end_log - cumul), values_in, ((0,), (0,)))
        state = column_of(jnp.exp(end_log), key_dim)[:, :1] * state + added
        before = before + end_log
    pair_ref[:, :value_dim] = state
    pair_ref[:, value_dim:] = column_of(jnp.exp(before), key_dim)


def gla_outputs(proj, cumuls_ref, states_ref, out_ref, decayed_ref):
    tokens, key_dim = cumuls_ref.shape
    value_dim = states_ref.shape[2]
    causal = triangle(BLOCK)
    before = jnp.zeros((1, key_dim), jnp.float32)
    for block in range(tokens // BLOCK):
        span = pl.ds(block * BLOCK, BLOCK)
        queries = proj[span, :key_dim]
        keys_in = proj[span, key_dim : 2 * key_dim]
        values_in = proj[span, 2 * key_dim : 2 * key_dim + value_dim]
        cumul = cumuls_ref[span, :]
        end_log = cumul[BLOCK - 1 :, :]
        anchor = 0.5 * end_log
        scores = hdot(
            queries * jnp.exp(cumul - anchor), keys_in * jnp.exp(anchor - cumul), ((1,), (1,))
        )
        scores = jnp.where(causal, scores, 0.0)
        out_ref[span, :] = hdot(scores, values_in, ((1,), (0,))) + hdot(
            queries * jnp.exp(cumul), states_ref[block], ((1,), (0,))
        )
        decayed_ref[span, :] = queries * jnp.exp(cumul + before)
        before = before + end_log


def gla_backward(proj, cumuls_ref, states_ref, entry_ref, later_ref, g_ref, dqkv_ref, dr_ref):
    tokens, key_dim = cumuls_ref.shape
    value_dim = g_ref.shape[1]
    causal = triangle(BLOCK)
    ones_low = causal.astype(jnp.float32)
    blocks = tokens // BLOCK
    cumuls, befores = [], []
    before = jnp.zeros((1, key_dim), jnp.float32)
    for block in range(blocks):
        cumul = cumuls_ref[pl.ds(block * BLOCK, BLOCK), :]
        cumuls.append(cumul)
        befores.append(before)
        before = before + cumul[BLOCK - 1 :, :]
    grad_state = later_ref[...]
    entry = entry_ref[...]
    for block in reversed(range(blocks)):
        span = pl.ds(block * BLOCK, BLOCK)
        queries = proj[span, :key_dim]
        keys_in = proj[span, key_dim : 2 * key_dim]
        values_in = proj[span, 2 * key_dim : 2 * key_dim + value_dim]
        grad_out = g_ref[span, :]
        cumul = cumuls[block]
        end_log = cumul[BLOCK - 1 :, :]
        anchor = 0.5 * end_log
        state = states_ref[block] + column_of(jnp.exp(befores[block]), key_dim)[:, :1] * entry
        up, down = jnp.exp(cumul - anchor), jnp.exp(anchor - cumul)
        grow, rest = jnp.exp(cumul), jnp.exp(end_log - cumul)
        q_up, k_down = queries * up, keys_in * down
        scores = jnp.where(causal, hdot(q_up, k_down, ((1,), (1,))), 0.0)
        grad_scores = jnp.where(causal, hdot(grad_out, values_in, ((1,), (1,))), 0.0)
        grad_q = hdot(grad_scores, k_down, ((1,), (0,))) * up + grow * hdot(
            grad_out, state, ((1,), (1,))
        )
        carried_k = hdot(values_in, grad_state, ((1,), (1,))) * rest
        grad_k = hdot(grad_scores, q_up, ((0,), (0,))) * down + carried_k
        dqkv_ref[span, 2 * key_dim : 2 * key_dim + value_dim] = (
            hdot(scores, grad_out, ((0,), (0,)))
            + hdot(keys_in * rest, grad_state, ((1,), (0,)))
        ).astype(dqkv_ref.dtype)
        dqkv_ref[span, :key_dim] = (grad_q * key_dim ** (-0.5)).astype(dqkv_ref.dtype)
        dqkv_ref[span, key_dim : 2 * key_dim] = grad_k.astype(dqkv_ref.dtype)
        grad_cumul = queries * grad_q - keys_in * grad_k
        end_column = column_of(jnp.exp(end_log), key_dim)
        state_term = jnp.sum(grad_state * state, axis=1, keepdims=True) * end_column
        grad_end = state_term.T[:1, :] + jnp.sum(carried_k * keys_in, axis=0, keepdims=True)
        dr_ref[span, :] = hdot(ones_low, grad_cumul, ((0,), (0,))) + grad_end
        grad_state = end_column[:, :1] * grad_state + hdot(
            queries * grow, grad_out, ((0,), (0,))
        )


LOADS = ("x", "wq", "wk", "wv", "wgo", "wo", "g", "wd", "wg", "wu")


class Refs:
    def __init__(self, pairs):
        self.__dict__.update(pairs)

    def made(self, i):
        return getattr(self, "made%d" % i)

    def near(self, i):
        return getattr(self, "near%d" % i)

    def line(self, i):
        return getattr(self, "line%d" % i)

    def near_sem(self, i):
        return getattr(self, "near_sem%d" % i)

    def line_sem(self, i):
        return getattr(self, "line_sem%d" % i)

    def left(self, i):
        return getattr(self, "left%d" % i)


def mm_tn(left, right):
    return lax.dot_general(
        left, right, (((0,), (0,)), ((), ())), preferred_element_type=jnp.float32
    )


def block_kernel(sizes, names, pieces, wide, *refs):
    f32, bf16 = jnp.float32, jnp.bfloat16
    n_ctx, n_dp, n_ten = sizes
    R = Refs(zip(names, refs))
    ctx = lax.axis_index("context")
    dp = lax.axis_index("dp")
    ten = lax.axis_index("tensor")
    tokens, model = R.x_s.shape
    key_dim = R.wq.shape[1]
    value_dim = R.wv.shape[1]
    hidden = R.wg.shape[0]
    rank = R.wld.shape[0]
    own_rows = tokens // n_ten
    owners = n_ctx * n_dp
    part = model // owners
    last = n_dp - 1
    mine = pl.ds(pl.multiple_of(ten * own_rows, own_rows), own_rows)
    near_ten = ten + 1 - 2 * lax.rem(ten, 2)
    over_ten = lax.rem(ten + 2, 4)
    far_ten = lax.rem(near_ten + 2, 4)
    is_end = jnp.logical_or(dp == 0, dp == last)
    absorbs = jnp.logical_or(dp == 1, dp == last - 1)
    end_peer = jnp.where(dp == 0, 1, last - 1)
    absorb_peer = jnp.where(dp == 1, 0, last)

    def remote(src, dst, send, recv, axis, peer):
        return pltpu.make_async_remote_copy(
            src_ref=src,
            dst_ref=dst,
            send_sem=send,
            recv_sem=recv,
            device_id={axis: peer},
            device_id_type=MESH_ID,
        )

    spots = dict(
        x=R.x_s,
        wq=R.wcat.at[:, :key_dim],
        wk=R.wcat.at[:, key_dim : 2 * key_dim],
        wv=R.wcat.at[:, 2 * key_dim : 2 * key_dim + value_dim],
        wgo=R.wcat.at[:, 2 * key_dim + value_dim :],
        wo=R.wo_s,
        g=R.g_s.at[:tokens],
        wd=R.wd_s,
        wg=R.wgu.at[:hidden],
        wu=R.wgu.at[hidden:],
    )

    def load(name):
        return pltpu.make_async_copy(getattr(R, name), spots[name], R.load_sem.at[LOADS.index(name)])

    for name in LOADS:
        load(name).start()

    barrier = pltpu.get_barrier_semaphore()

    def greet(axis, peer):
        pl.semaphore_signal(barrier, inc=1, device_id={axis: peer}, device_id_type=MESH_ID)

    for step in range(1, n_ctx):
        greet("context", lax.rem(ctx + step, n_ctx))
    for step in range(1, n_ten):
        greet("tensor", lax.rem(ten + step, n_ten))

    @pl.when(dp > 0)
    def _():
        greet("dp", dp - 1)

    @pl.when(dp < last)
    def _():
        greet("dp", dp + 1)

    load("x").wait()
    rows_in = R.x_s[...].astype(f32)
    n1f = (rows_in * rms_scale(rows_in) * R.gain1[...]).astype(bf16)
    R.n1_s[...] = n1f
    for name in ("wq", "wk", "wv", "wgo"):
        load(name).wait()
    packed = mm(n1f, R.wcat[...])
    R.proj[:, :key_dim] = packed[:, :key_dim] * key_dim ** (-0.5)
    R.proj[:, key_dim:] = packed[:, key_dim:]
    low = mm_nt(n1f, R.wld[...])
    R.low[...] = low
    logits = hdot(low, R.wlu[...].astype(f32), ((1,), (0,))) + R.bias[...]
    R.logits[...] = logits
    R.rates[...] = (
        jnp.minimum(logits, 0.0) - jnp.log1p(jnp.exp(-jnp.abs(logits)))
    ) / GATE_NORM
    gla_states(R.proj, R.rates, R.cumuls, R.states, R.pair)

    expect = n_ctx + n_ten - 2

    @pl.when(jnp.logical_not(is_end))
    def _():
        pl.semaphore_wait(barrier, expect + 2)

    @pl.when(is_end)
    def _():
        pl.semaphore_wait(barrier, expect + 1)

    def ctx_copy(which, src, slots, step):
        return remote(
            src,
            slots.at[step - 1],
            R.ctx_sem.at[which, 0, step - 1],
            R.ctx_sem.at[which, 1, step - 1],
            "context",
            lax.rem(ctx + step, n_ctx),
        )

    def fold(out_ref, slots, reverse):
        out_ref[...] = jnp.zeros_like(out_ref)
        for m in reversed(range(1, n_ctx)):
            index = n_ctx - m - 1 if reverse else m - 1

            @pl.when(ctx + m < n_ctx if reverse else ctx >= m)
            def _(index=index):
                out_ref[...] = (
                    slots[index, :, value_dim : value_dim + 1] * out_ref[...]
                    + slots[index, :, :value_dim]
                )

    for step in range(1, n_ctx):
        ctx_copy(0, R.pair, R.pair_slots, step).start()

    load("g").wait()
    R.sum_src[1] = R.g_s[:tokens, :].astype(f32).reshape(R.sum_src.shape[1:])

    def ext_copy(which, peer):
        if which == 0:
            src, dst = R.sum_src.at[1], R.shared.at[2]
        else:
            src, dst = R.shared.at[0, ten], R.shared.at[3, ten]
        return remote(src, dst, R.ext_sem.at[which, 0], R.ext_sem.at[which, 1], "dp", peer)

    @pl.when(is_end)
    def _():
        ext_copy(0, end_peer).start()

    gla_outputs(R.proj, R.cumuls, R.states, R.o_s, R.decayed)
    for step in range(1, n_ctx):
        ctx_copy(0, R.pair, R.pair_slots, step).wait_recv()
    fold(R.entry, R.pair_slots, False)
    o = R.o_s[...] + hdot(R.decayed[...], R.entry[...], ((1,), (0,)))
    R.o_s[...] = o
    gate_in = R.proj[:, 2 * key_dim + value_dim :]
    scale_h = lax.rsqrt(jnp.mean(o * o, axis=-1, keepdims=True) + EPS_HEAD)
    gated = o * scale_h * R.hgain[...] * (gate_in * jax.nn.sigmoid(gate_in))
    load("wo").wait()

    def sum_copy(which, bank, n):
        src = R.sum_src
        source = (
            src.at[bank, far_ten, 0],
            src.at[bank, far_ten, 1],
            src.at[bank, near_ten, 0],
            src.at[bank, over_ten, 1],
            R.sum_via.at[bank, 0],
            R.sum_via.at[bank, 1],
        )[n]
        peer = (near_ten, over_ten, near_ten, over_ten, over_ten, near_ten)[n]
        return remote(
            source,
            R.sum_slots.at[bank, n],
            R.sum_sem.at[which, 0, n],
            R.sum_sem.at[which, 1, n],
            "tensor",
            peer,
        )

    def sum_start(which, bank, value):
        R.sum_src[bank] = value.reshape(n_ten, 2, own_rows // 2, model)
        for n in range(4):
            sum_copy(which, bank, n).start()

    def sum_relay(which, bank):
        sum_copy(which, bank, 0).wait_recv()
        R.sum_via[bank, 0] = R.sum_slots[bank, 0] + R.sum_src[bank, over_ten, 0]
        sum_copy(which, bank, 4).start()
        sum_copy(which, bank, 1).wait_recv()
        R.sum_via[bank, 1] = R.sum_slots[bank, 1] + R.sum_src[bank, near_ten, 1]
        sum_copy(which, bank, 5).start()

    def sum_end(which, bank):
        for n in range(2, 6):
            sum_copy(which, bank, n).wait_recv()
        slots = R.sum_slots
        own = R.sum_src
        return jnp.concatenate(
            [
                own[bank, ten, 0] + slots[bank, 2] + slots[bank, 4],
                own[bank, ten, 1] + slots[bank, 3] + slots[bank, 5],
            ],
            axis=0,
        )

    def sum_sent(which, bank):
        for n in range(6):
            sum_copy(which, bank, n).wait_send()

    def share_copy(which, n, arriving=False):
        if arriving:
            owner = (near_ten, over_ten, near_ten, over_ten, far_ten, far_ten)[n]
        else:
            owner = (ten, ten, ten, ten, near_ten, over_ten)[n]
        spot = R.shared.at[min(which, 3), owner, (0, 1, 1, 0, 0, 1)[n]]
        return remote(
            spot,
            spot,
            R.share_sem.at[which, 0, n],
            R.share_sem.at[which, 1, n],
            "tensor",
            (near_ten, over_ten, near_ten, over_ten, over_ten, near_ten)[n],
        )

    def share_start(which, value=None):
        if value is not None:
            R.shared[which, ten] = value.reshape(2, own_rows // 2, model)
        for n in range(4):
            share_copy(which, n).start()

    def share_relay(which):
        share_copy(which, 0, True).wait_recv()
        share_copy(which, 4).start()
        share_copy(which, 1, True).wait_recv()
        share_copy(which, 5).start()

    def share_end(which):
        for n in range(2, 6):
            share_copy(which, n, True).wait_recv()

    def share_sent(which):
        for n in range(6):
            share_copy(which, n).wait_send()

    arrays = len(pieces)
    cut = (1, 1, 0, 0, 0)
    heights = [R.made(i).shape[1] for i in range(arrays)]

    def rows(i, piece):
        height = heights[i] // pieces[i]
        return pl.ds(piece * height, height)

    def near_copy(i, step, dest, piece):
        peer = lax.rem(ctx + step, n_ctx)
        return remote(
            R.made(i).at[peer * n_dp + dest, rows(i, piece)],
            R.near(i).at[step - 1, dest, rows(i, piece)],
            R.near_sem(i).at[0, step - 1, dest, piece],
            R.near_sem(i).at[1, step - 1, dest, piece],
            "context",
            peer,
        )

    def line_copy(i, way, dest, piece, peer):
        goal = jnp.where(dest == peer, n_dp, dest) if way == 1 else dest
        return remote(
            R.line(i).at[dest, rows(i, piece)],
            R.line(i).at[goal, rows(i, piece)],
            R.line_sem(i).at[0, way, dest, piece],
            R.line_sem(i).at[1, way, dest, piece],
            "dp",
            peer,
        )

    def loop(low, high, body):
        if high - low == 1:
            body(low)
        else:

            def lap(index, carry):
                body(index)
                return carry

            lax.fori_loop(low, high, lap, 0)

    def over_pieces(i, body):
        loop(0, pieces[i], body)

    def over_steps(body):
        loop(1, n_ctx, body)

    def takes_part(i, dest):
        if not cut[i]:
            return True
        if dest == 0:
            return dp < last
        if dest == last:
            return dp > 0
        return jnp.logical_not(is_end)

    def guarded(condition, body):
        if condition is True:
            body()
        else:
            pl.when(condition)(body)

    def put(i, owner, dest):
        made = R.made(i)
        cols = pl.ds(pl.multiple_of(owner * part, part), part) if wide else None
        if i < 2:
            right = R.mixed if i == 0 else R.gpair
            left = R.g_s if i == 0 else R.n2_s
            both = jnp.logical_or(
                dp == 1 if dest >= 1 else False, dp == last - 1 if dest < last else False
            )

            @pl.when(both)
            def _():
                if wide:
                    made[owner] = mm(right[...], left[:, cols])
                else:
                    made[owner] = mm_nt(R.left(i)[owner], right[...])

            @pl.when(jnp.logical_not(both))
            def _():
                if wide:
                    made[owner] = mm(right[:, :tokens], left[:tokens, cols])
                else:
                    made[owner] = mm_nt(R.left(i)[owner, :, :tokens], right[:, :tokens])

        elif i == 2:
            if wide:
                made[owner] = mm(R.gated[...], R.n2_s[:tokens, cols])
            else:
                made[owner] = mm_nt(R.left0[owner, :, :tokens], R.gated[...])
        elif i == 3:
            made[owner] = mm(R.left3[owner], R.gproj[...])

    def make(i, dest):
        def body():
            def step_body(step):
                put(i, lax.rem(ctx + step, n_ctx) * n_dp + dest, dest)
                over_pieces(i, lambda piece: near_copy(i, step, dest, piece).start())

            over_steps(step_body)
            put(i, ctx * n_dp + dest, dest)

        guarded(takes_part(i, dest), body)

    def own_sum(i, dest, piece):
        total = R.made(i)[ctx * n_dp + dest, rows(i, piece)]
        for step in range(1, n_ctx):
            near_copy(i, step, dest, piece).wait_recv()
            total = total + R.near(i)[step - 1, dest, rows(i, piece)]
        return total

    def first_send(i, way, dest):
        start = cut[i] if way == 0 else last - cut[i]
        if dest <= start if way == 0 else dest >= start:
            return

        @pl.when(dp == start)
        def _():
            def body(piece):
                R.line(i)[dest, rows(i, piece)] = own_sum(i, dest, piece)
                line_copy(i, way, dest, piece, dp + 1 if way == 0 else dp - 1).start()

            over_pieces(i, body)

    def middle_send(i, way, dest, hop):
        reach = dest - cut[i] if way == 0 else last - cut[i] - dest
        if reach < (2 if hop == 1 else 3):
            return
        if way == 0:
            active = dp == cut[i] + 1
            if hop > 1:
                active = jnp.logical_and(dp > cut[i] + 1, dp < dest)
        else:
            active = dp == last - cut[i] - 1
            if hop > 1:
                active = jnp.logical_and(dp < last - cut[i] - 1, dp > dest)
        peer = dp + 1 if way == 0 else dp - 1

        @pl.when(active)
        def _():
            def body(piece):
                own = own_sum(i, dest, piece)
                line_copy(i, way, dest, piece, dp).wait_recv()
                R.line(i)[dest, rows(i, piece)] = (
                    R.line(i)[dest, rows(i, piece)] + own
                )
                line_copy(i, way, dest, piece, peer).start()

            over_pieces(i, body)

    def makes(i, k):
        for dest in dict.fromkeys((last - k, k)):
            make(i, dest)

    def firsts(i, k):
        first_send(i, 0, last - k)
        first_send(i, 1, k)

    def middles(i, k, hop):
        middle_send(i, 0, last - k, hop)
        middle_send(i, 1, k, hop)

    laps = -(-n_dp // 2)

    def build(i, begin=0):
        for k in range(begin, laps):
            makes(i, k)
            firsts(i, k)
        for k in range(laps, last):
            firsts(i, k)

    def finish(i, out):
        def body(piece):
            span = rows(i, piece)
            here = ctx * n_dp + dp
            made = R.made(i)
            made[here, span] = own_sum(i, dp, piece)

            @pl.when(dp > cut[i])
            def _():
                line_copy(i, 0, dp, piece, dp).wait_recv()
                made[here, span] += R.line(i)[dp, span]

            @pl.when(dp < last - cut[i])
            def _():
                line_copy(i, 1, dp, piece, dp).wait_recv()
                made[here, span] += R.line(i)[n_dp, span]

            out(span, made[here, span])

        over_pieces(i, body)

    def drain(i):
        for dest in range(n_dp):

            def near_sent(dest=dest):
                def body(piece):
                    for step in range(1, n_ctx):
                        near_copy(i, step, dest, piece).wait_send()

                over_pieces(i, body)

            guarded(takes_part(i, dest), near_sent)
            if dest > cut[i]:

                @pl.when(jnp.logical_and(dp >= cut[i], dp < dest))
                def _(dest=dest):
                    over_pieces(
                        i, lambda piece: line_copy(i, 0, dest, piece, dp + 1).wait_send()
                    )

            if dest < last - cut[i]:

                @pl.when(jnp.logical_and(dp <= last - cut[i], dp > dest))
                def _(dest=dest):
                    over_pieces(
                        i, lambda piece: line_copy(i, 1, dest, piece, dp - 1).wait_send()
                    )

    def turned(value):
        return value.T.reshape(owners, part, value.shape[0]).astype(bf16)

    sum_start(0, 0, mm(gated.astype(bf16), R.wo_s[...]))
    R.gated[...] = gated.T.astype(bf16)
    R.left3[...] = turned(R.n1_s[...].astype(f32))
    load("wd").wait()
    R.gm[...] = mm_nt(R.wd_s[...], R.g_s[:tokens, :])
    sum_relay(0, 0)
    hid = R.x_s[mine, :].astype(f32) + sum_end(0, 0)
    R.hid[...] = hid
    gain2 = R.gain2[...]
    share_start(0, (hid * rms_scale(hid) * gain2).astype(bf16).astype(f32))

    @pl.when(is_end)
    def _():
        ext_copy(1, end_peer).start()

    load("wg").wait()
    load("wu").wait()
    sum_sent(0, 0)
    share_relay(0)

    @pl.when(absorbs)
    def _():
        ext_copy(0, absorb_peer).wait_recv()
        R.g_s[tokens:, :] = R.shared[2].reshape(tokens, model).astype(bf16)
        ext_copy(1, absorb_peer).wait_recv()
        share_start(4)

    share_end(0)

    def feed_forward(half, grad_mixed):
        span = slice(half * tokens, (half + 1) * tokens)
        n2 = R.n2_s[span, :]
        ffn_gate = mm_nt(R.wgu[:hidden, :], n2)
        ffn_up = mm_nt(R.wgu[hidden:, :], n2)
        sig = jax.nn.sigmoid(ffn_gate)
        soft = ffn_gate * sig
        R.mixed[:, span] = (soft * ffn_up).astype(bf16)
        R.gpair[:hidden, span] = (
            grad_mixed * ffn_up * (sig * (1.0 + ffn_gate * (1.0 - sig)))
        ).astype(bf16)
        R.gpair[hidden:, span] = (grad_mixed * soft).astype(bf16)

    R.n2_s[:tokens, :] = R.shared[0].reshape(tokens, model).astype(bf16)
    feed_forward(0, R.gm[...])

    @pl.when(absorbs)
    def _():
        share_relay(4)

    sum_start(1, 0, mm_tn(R.gpair[:, :tokens], R.wgu[...]))

    @pl.when(absorbs)
    def _():
        R.gm[...] = mm_nt(R.wd_s[...], R.g_s[tokens:, :])

    sum_relay(1, 0)

    @pl.when(absorbs)
    def _():
        share_end(4)
        R.n2_s[tokens:, :] = R.shared[3].reshape(tokens, model).astype(bf16)
        feed_forward(1, R.gm[...])

    if not wide:
        for at in range(0, 2 * tokens, 128):
            span = slice(at, at + 128)
            R.left0[:, :, span] = turned(R.g_s[span, :].astype(f32))
            R.left1[:, :, span] = turned(R.n2_s[span, :].astype(f32))
    makes(0, 0)
    firsts(0, 0)
    grad_normed_two = sum_end(1, 0)
    hid = R.hid[...]
    grad_two_rows, gain_two_part = norm_back(hid, rms_scale(hid), gain2, grad_normed_two)
    grad_hidden = R.g_s[mine, :].astype(f32) + grad_two_rows
    R.gh[...] = grad_hidden
    share_start(1, grad_hidden.astype(bf16).astype(f32))
    sum_sent(1, 0)
    build(0, 1)
    share_relay(1)

    @pl.when(is_end)
    def _():
        ext_copy(0, end_peer).wait_send()

    sum_start(2, 1, mm_tn(R.mixed[:, :tokens], R.wd_s[...]))
    build(1)
    middles(0, 0, 1)
    share_end(1)

    R.n2_s[:tokens, :] = R.shared[1].reshape(tokens, model).astype(bf16)
    grad_gated = mm_nt(R.n2_s[:tokens, :], R.wo_s[...])
    o = R.o_s[...]
    gate_in = R.proj[:, 2 * key_dim + value_dim :]
    scale_h = lax.rsqrt(jnp.mean(o * o, axis=-1, keepdims=True) + EPS_HEAD)
    sig = jax.nn.sigmoid(gate_in)
    soft = gate_in * sig
    hgain = R.hgain[...]
    normal = o * scale_h
    head_part = jnp.sum(grad_gated * normal * soft, axis=0, keepdims=True)
    R.gproj[:, 2 * key_dim + value_dim :] = (
        grad_gated * normal * hgain * (sig * (1.0 + gate_in * (1.0 - sig)))
    ).astype(bf16)
    back = grad_gated * hgain * soft
    go = scale_h * (
        back - normal * scale_h * jnp.mean(back * o, axis=-1, keepdims=True)
    )
    R.go[...] = go
    R.pair_back[:, :value_dim] = hdot(R.decayed[...], go, ((0,), (0,)))
    R.pair_back[:, value_dim:] = R.pair[:, value_dim:]
    for step in range(1, n_ctx):
        ctx_copy(1, R.pair_back, R.back_slots, step).start()
    sum_relay(2, 1)
    if not wide:
        R.left0[:, :, :tokens] = turned(R.shared[1].reshape(tokens, model))
    build(2)
    for step in range(1, n_ctx):
        ctx_copy(1, R.pair_back, R.back_slots, step).wait_recv()
    fold(R.later, R.back_slots, True)
    gla_backward(
        R.proj, R.cumuls, R.states, R.entry, R.later, R.go, R.gproj, R.dr
    )
    grad_logits = R.dr[...] * jax.nn.sigmoid(-R.logits[...]) / GATE_NORM
    grad_low = hdot(grad_logits, R.wlu[...].astype(f32), ((1,), (1,)))

    @pl.when(absorbs)
    def _():
        share_sent(4)

    sum_start(
        3,
        0,
        mm_nt(R.gproj[...], R.wcat[...])
        + hdot(grad_low, R.wld[...].astype(f32), ((1,), (0,))),
    )
    low_down = hdot(grad_low, R.n1_s[...].astype(f32), ((0,), (0,)))
    low_up = hdot(R.low[...], grad_logits, ((0,), (0,)))
    bias_part = jnp.sum(grad_logits, axis=0, keepdims=True)
    rows_in = R.x_s[...].astype(f32)
    gain_one_part = jnp.sum(
        R.sum_src[0].reshape(tokens, model) * (rows_in * rms_scale(rows_in)),
        axis=0,
        keepdims=True,
    )
    R.made4[...] = jnp.zeros_like(R.made4)
    part_head = value_dim // owners
    part_key = key_dim // owners
    tail = R.tail_slots.shape[1]
    for owner in range(owners):
        span = slice(owner * part, (owner + 1) * part)
        R.made4[owner, :rank, :part] = low_down[:, span]
        R.made4[owner, rank : rank + 1, :part] = gain_one_part[:, span]
        R.made4[owner, rank + 1 : rank + 2, :part] = gain_two_part[:, span]
        R.made4[owner, rank + 2 : rank + 3, :part_head] = head_part[
            :, owner * part_head : (owner + 1) * part_head
        ]
        span = slice(owner * part_key, (owner + 1) * part_key)
        R.made4[owner, tail : tail + rank, :part_key] = low_up[:, span]
        R.made4[owner, tail + rank : tail + rank + 1, :part_key] = bias_part[:, span]
    build(4)
    build(3)
    sum_relay(3, 0)
    for k in range(last):
        middles(2, k, 1)
    for k in range(last):
        middles(4, k, 1)
    middles(1, 0, 1)
    result = R.hid[...] + sum_end(2, 1)
    share_start(2, result.astype(bf16).astype(f32))
    middles(3, 0, 1)
    grad_normed_one = sum_end(3, 0)
    own_in = R.x_s[mine, :].astype(f32)
    grad_one_rows, _ = norm_back(own_in, rms_scale(own_in), R.gain1[...], grad_normed_one)
    share_relay(2)
    share_start(3, R.gh[...] + grad_one_rows)
    for i in range(2):
        for k in range(1, last):
            middles(i, k, 1)
    for k in range(1, last):
        middles(3, k, 1)
    share_relay(3)
    for i in (0, 1, 2, 4, 3):
        for k in range(last):
            middles(i, k, 2)

    def into(name):
        def out(span, value):
            getattr(R, name)[span, :] = value

        return out

    def put_proj(span, value):
        R.gq[span, :] = value[:, :key_dim]
        R.gk[span, :] = value[:, key_dim : 2 * key_dim]
        R.gv[span, :] = value[:, 2 * key_dim : 2 * key_dim + value_dim]
        R.ggo[span, :] = value[:, 2 * key_dim + value_dim :]

    finish(0, into("gdown"))
    finish(1, into("gpairs"))
    share_end(2)
    R.result[...] = R.shared[2].reshape(tokens, model).astype(bf16)
    finish(2, into("gout"))
    finish(4, into("pack"))
    R.tail_slots[ten] = R.pack[:tail, :]

    def tail_copy(sender, peer, step):
        spot = R.tail_slots.at[sender]
        return remote(
            spot, spot, R.tail_sem.at[0, step - 1], R.tail_sem.at[1, step - 1], "tensor", peer
        )

    for step in range(1, n_ten):
        tail_copy(ten, lax.rem(ten + step, n_ten), step).start()
    finish(3, put_proj)
    share_end(3)
    R.gin[...] = R.shared[3].reshape(tokens, model)
    for step in range(1, n_ten):
        sender = lax.rem(ten + n_ten - step, n_ten)
        tail_copy(sender, sender, step).wait_recv()
    total = R.tail_slots[0]
    for index in range(1, n_ten):
        total = total + R.tail_slots[index]
    R.pack[:tail, :] = total

    for step in range(1, n_ctx):
        ctx_copy(0, R.pair, R.pair_slots, step).wait_send()
        ctx_copy(1, R.pair_back, R.back_slots, step).wait_send()
    sum_sent(2, 1)
    sum_sent(3, 0)
    for which in range(4):
        share_sent(which)

    @pl.when(is_end)
    def _():
        ext_copy(1, end_peer).wait_send()

    for i in range(arrays):
        drain(i)
    for step in range(1, n_ten):
        tail_copy(ten, lax.rem(ten + step, n_ten), step).wait_send()


def hand_out_kernel(moves, n_in, n_big, *refs):
    ins, pack_ref = refs[: n_in - 1], refs[n_in - 1]
    big = refs[n_in : n_in + n_big]
    small = refs[n_in + n_big : -1]
    sems = refs[-1]
    copies = []
    for at, (source, first, rows) in enumerate(moves):
        src = ins[source] if rows is None else ins[source].at[first : first + rows]
        copies.append(pltpu.make_async_copy(src, big[at], sems.at[at]))
        copies[-1].start()
    low_down, gain1, gain2, hgain, low_up, bias = small
    rank, part = low_down.shape
    tail = -(-(rank + 3) // 8) * 8
    low_down[...] = pack_ref[:rank, :part]
    gain1[...] = pack_ref[rank : rank + 1, :part]
    gain2[...] = pack_ref[rank + 1 : rank + 2, :part]
    hgain[...] = pack_ref[rank + 2 : rank + 3, : hgain.shape[1]]
    low_up[...] = pack_ref[tail : tail + rank, : low_up.shape[1]]
    bias[...] = pack_ref[tail + rank : tail + rank + 1, : bias.shape[1]]
    for copy in copies:
        copy.wait()


def shards(
    inputs,
    norm_gain1,
    w_query,
    w_key,
    w_value,
    w_gate_out,
    w_low_down,
    w_low_up,
    forget_bias,
    head_gain,
    w_output,
    norm_gain2,
    w_ffn_gate,
    w_ffn_up,
    w_ffn_down,
    cotangent,
):
    bf16, f32 = jnp.bfloat16, jnp.float32
    n_ctx, n_dp, n_ten = (lax.axis_size(axis) for axis in ("context", "dp", "tensor"))
    owners = n_ctx * n_dp
    model = inputs.shape[-1]
    x = inputs.reshape(-1, model)
    tokens = x.shape[0]
    key_dim, value_dim, hidden = w_query.shape[1], w_value.shape[1], w_ffn_gate.shape[1]
    assert inputs.shape[0] == 1 and head_gain.shape[0] == value_dim
    assert n_ten == 4 and n_dp >= 4
    rank = w_low_down.shape[1]
    part = model // owners
    wide = part % 128 == 0
    own_rows = tokens // n_ten
    width = 2 * key_dim + 2 * value_dim
    tail = -(-(rank + 3) // 8) * 8
    pack_rows = tail + -(-(rank + 1) // 8) * 8

    ins = dict(
        x=x,
        gain1=norm_gain1[None],
        wq=w_query,
        wk=w_key,
        wv=w_value,
        wgo=w_gate_out,
        wld=w_low_down.T,
        wlu=w_low_up,
        bias=forget_bias[None],
        hgain=head_gain[None],
        wo=w_output,
        gain2=norm_gain2[None],
        wg=w_ffn_gate.T,
        wu=w_ffn_up.T,
        wd=w_ffn_down,
        g=cotangent.reshape(-1, model),
    )

    def owned(extent):
        return (extent, part) if wide else (part, extent)

    shapes = [owned(hidden), owned(2 * hidden), owned(value_dim), (part, width), (pack_rows, 128)]
    outs = dict(
        result=((tokens, model), bf16),
        gin=((tokens, model), f32),
        gq=((part, key_dim), f32),
        gk=((part, key_dim), f32),
        gv=((part, value_dim), f32),
        ggo=((part, value_dim), f32),
        gout=(shapes[2], f32),
        gpairs=(shapes[1], f32),
        gdown=(shapes[0], f32),
        pack=((pack_rows, 128), f32),
    )
    pieces = []
    for shape in shapes:
        count = 4
        while shape[0] % (count * 8):
            count //= 2
        pieces.append(count if shape[0] * shape[1] > 16384 else 1)

    dma = pltpu.SemaphoreType.DMA
    scratch = dict(
        x_s=pltpu.VMEM((tokens, model), bf16),
        g_s=pltpu.VMEM((2 * tokens, model), bf16),
        ext_sem=dma((2, 2)),
        wcat=pltpu.VMEM((model, width), bf16),
        wo_s=pltpu.VMEM((value_dim, model), bf16),
        wgu=pltpu.VMEM((2 * hidden, model), bf16),
        wd_s=pltpu.VMEM((hidden, model), bf16),
        load_sem=dma((len(LOADS),)),
        n1_s=pltpu.VMEM((tokens, model), bf16),
        n2_s=pltpu.VMEM((2 * tokens, model), bf16),
        proj=pltpu.VMEM((tokens, width), f32),
        low=pltpu.VMEM((tokens, rank), f32),
        logits=pltpu.VMEM((tokens, key_dim), f32),
        rates=pltpu.VMEM((tokens, key_dim), f32),
        cumuls=pltpu.VMEM((tokens, key_dim), f32),
        o_s=pltpu.VMEM((tokens, value_dim), f32),
        decayed=pltpu.VMEM((tokens, key_dim), f32),
        states=pltpu.VMEM((tokens // BLOCK, key_dim, value_dim), f32),
        pair=pltpu.VMEM((key_dim, value_dim + key_dim), f32),
        pair_back=pltpu.VMEM((key_dim, value_dim + key_dim), f32),
        pair_slots=pltpu.VMEM((n_ctx - 1, key_dim, value_dim + key_dim), f32),
        back_slots=pltpu.VMEM((n_ctx - 1, key_dim, value_dim + key_dim), f32),
        ctx_sem=dma((2, 2, n_ctx - 1)),
        entry=pltpu.VMEM((key_dim, value_dim), f32),
        later=pltpu.VMEM((key_dim, value_dim), f32),
        gm=pltpu.VMEM((hidden, tokens), f32),
        gated=pltpu.VMEM((value_dim, tokens), bf16),
        sum_src=pltpu.VMEM((2, n_ten, 2, own_rows // 2, model), f32),
        sum_slots=pltpu.VMEM((2, 6, own_rows // 2, model), f32),
        sum_via=pltpu.VMEM((2, 2, own_rows // 2, model), f32),
        sum_sem=dma((4, 2, 6)),
        shared=pltpu.VMEM((4, n_ten, 2, own_rows // 2, model), f32),
        share_sem=dma((5, 2, 6)),
        hid=pltpu.VMEM((own_rows, model), f32),
        gh=pltpu.VMEM((own_rows, model), f32),
        mixed=pltpu.VMEM((hidden, 2 * tokens), bf16),
        gpair=pltpu.VMEM((2 * hidden, 2 * tokens), bf16),
        go=pltpu.VMEM((tokens, value_dim), f32),
        dr=pltpu.VMEM((tokens, key_dim), f32),
        gproj=pltpu.VMEM((tokens, width), bf16),
        tail_slots=pltpu.VMEM((n_ten, tail, 128), f32),
        tail_sem=dma((2, n_ten - 1)),
        left3=pltpu.VMEM((owners, part, tokens), bf16),
    )
    if not wide:
        scratch["left0"] = pltpu.VMEM((owners, part, 2 * tokens), bf16)
        scratch["left1"] = pltpu.VMEM((owners, part, 2 * tokens), bf16)
    for i, shape in enumerate(shapes):
        scratch["made%d" % i] = pltpu.VMEM((owners,) + shape, f32)
        scratch["near%d" % i] = pltpu.VMEM((n_ctx - 1, n_dp) + shape, f32)
        scratch["line%d" % i] = pltpu.VMEM((n_dp + 1,) + shape, f32)
        scratch["near_sem%d" % i] = dma((2, n_ctx - 1, n_dp, pieces[i]))
        scratch["line_sem%d" % i] = dma((2, 2, n_dp, pieces[i]))

    names = tuple(ins) + tuple(outs) + tuple(scratch)
    made = pl.pallas_call(
        functools.partial(block_kernel, (n_ctx, n_dp, n_ten), names, tuple(pieces), wide),
        out_shape=tuple(jax.ShapeDtypeStruct(shape, kind) for shape, kind in outs.values()),
        in_specs=[
            pl.BlockSpec(memory_space=pl.ANY if name in LOADS else VMEM) for name in ins
        ],
        out_specs=tuple([pl.BlockSpec(memory_space=VMEM)] * len(outs)),
        scratch_shapes=list(scratch.values()),
        compiler_params=pltpu.CompilerParams(
            collective_id=0, has_side_effects=True, vmem_limit_bytes=VMEM_LIMIT
        ),
        name="gla_block",
    )(*ins.values())
    part_head = value_dim // owners
    part_key = key_dim // owners
    moves, big_shapes = [], []
    for at, name in enumerate(list(outs)[:-1]):
        shape, kind = outs[name]
        if name == "gpairs" and wide:
            for half in range(2):
                moves.append((at, half * hidden, hidden))
                big_shapes.append(((hidden, part), kind))
        else:
            moves.append((at, 0, None))
            big_shapes.append((shape, kind))
    small_shapes = [
        (rank, part),
        (1, part),
        (1, part),
        (1, part_head),
        (rank, part_key),
        (1, part_key),
    ]
    done = pl.pallas_call(
        functools.partial(hand_out_kernel, tuple(moves), len(made), len(moves)),
        out_shape=tuple(
            [jax.ShapeDtypeStruct(shape, kind) for shape, kind in big_shapes]
            + [jax.ShapeDtypeStruct(shape, f32) for shape in small_shapes]
        ),
        in_specs=[pl.BlockSpec(memory_space=VMEM)] * len(made),
        out_specs=tuple(
            [pl.BlockSpec(memory_space=pl.ANY)] * len(moves)
            + [pl.BlockSpec(memory_space=VMEM)] * len(small_shapes)
        ),
        scratch_shapes=[dma((len(moves),))],
        name="hand_out",
    )(*made)
    low_down, gain1, gain2, hgain, low_up, bias = done[len(moves) :]
    result, gin, gq, gk, gv, ggo, gout = done[:7]
    if wide:
        ggate, gup, gdown = done[7].T, done[8].T, done[9]
    else:
        ggate, gup = done[7][:, :hidden], done[7][:, hidden:]
        gdown, gout = done[8].T, gout.T
    return (
        result.reshape(inputs.shape),
        gin.reshape(inputs.shape),
        gain1.reshape(-1),
        gq,
        gk,
        gv,
        ggo,
        low_down.T,
        low_up,
        bias.reshape(-1),
        hgain.reshape(-1),
        gout,
        gain2.reshape(-1),
        ggate,
        gup,
        gdown,
    )


def solution(mesh):
    return jax.shard_map(
        shards,
        mesh=mesh,
        in_specs=(
            P("dp", "context", None),
            P(),
            P(None, "tensor"),
            P(None, "tensor"),
            P(None, "tensor"),
            P(None, "tensor"),
            P(),
            P(None, "tensor"),
            P("tensor"),
            P(),
            P("tensor", None),
            P(),
            P(None, "tensor"),
            P(None, "tensor"),
            P("tensor", None),
            P("dp", "context", None),
        ),
        out_specs=(
            P("dp", "context", None),
            P("dp", "context", None),
            P(("context", "dp")),
            P(("context", "dp"), "tensor"),
            P(("context", "dp"), "tensor"),
            P(("context", "dp"), "tensor"),
            P(("context", "dp"), "tensor"),
            P(("context", "dp"), None),
            P(None, ("tensor", "context", "dp")),
            P(("tensor", "context", "dp")),
            P(("context", "dp")),
            P("tensor", ("context", "dp")),
            P(("context", "dp")),
            P(("context", "dp"), "tensor"),
            P(("context", "dp"), "tensor"),
            P("tensor", ("context", "dp")),
        ),
        check_vma=False,
    )
```

```python
import functools

import jax
import jax.numpy as jnp
from jax import lax
from jax.experimental import pallas as pl
from jax.experimental.pallas import tpu as pltpu
from jax.sharding import PartitionSpec as P

BLOCK = 64


EPS_MODEL = 1e-06
EPS_HEAD = 1e-05
GATE_NORM = 16.0
HIGHEST = lax.Precision.HIGHEST


VMEM_LIMIT = 63 * 1024 * 1024
VMEM = pltpu.MemorySpace.VMEM
MESH_ID = pl.DeviceIdType.MESH


def hdot(left, right, dims):
    return lax.dot_general(
        left, right, (dims, ((), ())), precision=HIGHEST, preferred_element_type=jnp.float32
    )


def hdot3(left, right, dims):
    f32, bf16 = jnp.float32, jnp.bfloat16

    def halves(value):
        high = value.astype(bf16)
        return high, (value - high.astype(f32)).astype(bf16)

    def dot(one, two):
        return lax.dot_general(one, two, (dims, ((), ())), preferred_element_type=f32)

    (left_high, left_low), (right_high, right_low) = halves(left), halves(right)
    return dot(left_high, right_high) + (dot(left_high, right_low) + dot(left_low, right_high))


def mm(left, right):
    return jnp.dot(left, right, preferred_element_type=jnp.float32)


def mm_nt(left, right):
    return lax.dot_general(
        left, right, (((1,), (1,)), ((), ())), preferred_element_type=jnp.float32
    )


def column_of(row, height):
    return jnp.broadcast_to(row, (height, row.shape[1])).T


def triangle(length):
    rows = lax.broadcasted_iota(jnp.int32, (length, length), 0)
    cols = lax.broadcasted_iota(jnp.int32, (length, length), 1)
    return rows >= cols


def rms_scale(rows_in):
    return lax.rsqrt(jnp.mean(rows_in * rows_in, axis=-1, keepdims=True) + EPS_MODEL)


def norm_back(rows_in, scale_rows, gain_in, grad_normed):
    weighted = gain_in * grad_normed
    grad_gain = jnp.sum(grad_normed * rows_in * scale_rows, axis=0, keepdims=True)
    grad_rows = scale_rows * (
        weighted
        - rows_in * scale_rows * scale_rows * jnp.mean(weighted * rows_in, axis=-1, keepdims=True)
    )
    return (grad_rows, grad_gain)


def gla_states(proj, rates, cumuls_ref, states_ref, pair_ref):
    tokens, key_dim = rates.shape
    value_dim = states_ref.shape[2]
    ones_low = triangle(BLOCK).astype(jnp.float32)
    state = jnp.zeros((key_dim, value_dim), jnp.float32)
    before = jnp.zeros((1, key_dim), jnp.float32)
    for block in range(tokens // BLOCK):
        span = pl.ds(block * BLOCK, BLOCK)
        keys_in = proj[span, key_dim : 2 * key_dim]
        values_in = proj[span, 2 * key_dim : 2 * key_dim + value_dim]
        cumul = hdot(ones_low, rates[span, :], ((1,), (0,)))
        cumuls_ref[span, :] = cumul
        end_log = cumul[BLOCK - 1 :, :]
        states_ref[block] = state
        added = hdot3(keys_in * jnp.exp(end_log - cumul), values_in, ((0,), (0,)))
        state = column_of(jnp.exp(end_log), key_dim)[:, :1] * state + added
        before = before + end_log
    pair_ref[:, :value_dim] = state
    pair_ref[:, value_dim:] = column_of(jnp.exp(before), key_dim)


def gla_outputs(proj, cumuls_ref, states_ref, out_ref, decayed_ref):
    tokens, key_dim = cumuls_ref.shape
    value_dim = states_ref.shape[2]
    causal = triangle(BLOCK)
    before = jnp.zeros((1, key_dim), jnp.float32)
    for block in range(tokens // BLOCK):
        span = pl.ds(block * BLOCK, BLOCK)
        queries = proj[span, :key_dim]
        keys_in = proj[span, key_dim : 2 * key_dim]
        values_in = proj[span, 2 * key_dim : 2 * key_dim + value_dim]
        cumul = cumuls_ref[span, :]
        end_log = cumul[BLOCK - 1 :, :]
        anchor = 0.5 * end_log
        scores = hdot3(
            queries * jnp.exp(cumul - anchor), keys_in * jnp.exp(anchor - cumul), ((1,), (1,))
        )
        scores = jnp.where(causal, scores, 0.0)
        out_ref[span, :] = hdot3(scores, values_in, ((1,), (0,))) + hdot3(
            queries * jnp.exp(cumul), states_ref[block], ((1,), (0,))
        )
        decayed_ref[span, :] = queries * jnp.exp(cumul + before)
        before = before + end_log


def gla_backward(proj, cumuls_ref, states_ref, entry_ref, later_ref, g_ref, dqkv_ref, dr_ref):
    tokens, key_dim = cumuls_ref.shape
    value_dim = g_ref.shape[1]
    causal = triangle(BLOCK)
    ones_low = causal.astype(jnp.float32)
    blocks = tokens // BLOCK
    cumuls, befores = [], []
    before = jnp.zeros((1, key_dim), jnp.float32)
    for block in range(blocks):
        cumul = cumuls_ref[pl.ds(block * BLOCK, BLOCK), :]
        cumuls.append(cumul)
        befores.append(before)
        before = before + cumul[BLOCK - 1 :, :]
    grad_state = later_ref[...]
    entry = entry_ref[...]
    for block in reversed(range(blocks)):
        span = pl.ds(block * BLOCK, BLOCK)
        queries = proj[span, :key_dim]
        keys_in = proj[span, key_dim : 2 * key_dim]
        values_in = proj[span, 2 * key_dim : 2 * key_dim + value_dim]
        grad_out = g_ref[span, :]
        cumul = cumuls[block]
        end_log = cumul[BLOCK - 1 :, :]
        anchor = 0.5 * end_log
        state = states_ref[block] + column_of(jnp.exp(befores[block]), key_dim)[:, :1] * entry
        up, down = jnp.exp(cumul - anchor), jnp.exp(anchor - cumul)
        grow, rest = jnp.exp(cumul), jnp.exp(end_log - cumul)
        q_up, k_down = queries * up, keys_in * down
        scores = jnp.where(causal, hdot(q_up, k_down, ((1,), (1,))), 0.0)
        grad_scores = jnp.where(causal, hdot(grad_out, values_in, ((1,), (1,))), 0.0)
        grad_q = hdot(grad_scores, k_down, ((1,), (0,))) * up + grow * hdot(
            grad_out, state, ((1,), (1,))
        )
        carried_k = hdot(values_in, grad_state, ((1,), (1,))) * rest
        grad_k = hdot(grad_scores, q_up, ((0,), (0,))) * down + carried_k
        dqkv_ref[span, 2 * key_dim : 2 * key_dim + value_dim] = (
            hdot(scores, grad_out, ((0,), (0,)))
            + hdot(keys_in * rest, grad_state, ((1,), (0,)))
        ).astype(dqkv_ref.dtype)
        dqkv_ref[span, :key_dim] = (grad_q * key_dim ** (-0.5)).astype(dqkv_ref.dtype)
        dqkv_ref[span, key_dim : 2 * key_dim] = grad_k.astype(dqkv_ref.dtype)
        grad_cumul = queries * grad_q - keys_in * grad_k
        end_column = column_of(jnp.exp(end_log), key_dim)
        state_term = jnp.sum(grad_state * state, axis=1, keepdims=True) * end_column
        grad_end = state_term.T[:1, :] + jnp.sum(carried_k * keys_in, axis=0, keepdims=True)
        dr_ref[span, :] = hdot(ones_low, grad_cumul, ((0,), (0,))) + grad_end
        grad_state = end_column[:, :1] * grad_state + hdot(
            queries * grow, grad_out, ((0,), (0,))
        )


LOADS = ("x", "wq", "wk", "wv", "wgo", "wo", "g", "wd", "wg", "wu")


class Refs:
    def __init__(self, pairs):
        self.__dict__.update(pairs)

    def made(self, i):
        return getattr(self, "made%d" % i)

    def near(self, i):
        return getattr(self, "near%d" % i)

    def line(self, i):
        return getattr(self, "line%d" % i)

    def near_sem(self, i):
        return getattr(self, "near_sem%d" % i)

    def line_sem(self, i):
        return getattr(self, "line_sem%d" % i)

    def left(self, i):
        return getattr(self, "left%d" % i)


def mm_tn(left, right):
    return lax.dot_general(
        left, right, (((0,), (0,)), ((), ())), preferred_element_type=jnp.float32
    )


def block_kernel(sizes, names, pieces, wide, *refs):
    f32, bf16 = jnp.float32, jnp.bfloat16
    n_ctx, n_dp, n_ten = sizes
    R = Refs(zip(names, refs))
    ctx = lax.axis_index("context")
    dp = lax.axis_index("dp")
    ten = lax.axis_index("tensor")
    tokens, model = R.x_s.shape
    key_dim = R.wq.shape[1]
    value_dim = R.wv.shape[1]
    hidden = R.wg.shape[0]
    rank = R.wld.shape[0]
    own_rows = tokens // n_ten
    owners = n_ctx * n_dp
    part = model // owners
    last = n_dp - 1
    mine = pl.ds(pl.multiple_of(ten * own_rows, own_rows), own_rows)
    near_ten = ten + 1 - 2 * lax.rem(ten, 2)
    over_ten = lax.rem(ten + 2, 4)
    far_ten = lax.rem(near_ten + 2, 4)
    is_end = jnp.logical_or(dp == 0, dp == last)
    absorbs = jnp.logical_or(dp == 1, dp == last - 1)
    end_peer = jnp.where(dp == 0, 1, last - 1)
    absorb_peer = jnp.where(dp == 1, 0, last)

    def remote(src, dst, send, recv, axis, peer):
        return pltpu.make_async_remote_copy(
            src_ref=src,
            dst_ref=dst,
            send_sem=send,
            recv_sem=recv,
            device_id={axis: peer},
            device_id_type=MESH_ID,
        )

    spots = dict(
        x=R.x_s,
        wq=R.wcat.at[:, :key_dim],
        wk=R.wcat.at[:, key_dim : 2 * key_dim],
        wv=R.wcat.at[:, 2 * key_dim : 2 * key_dim + value_dim],
        wgo=R.wcat.at[:, 2 * key_dim + value_dim :],
        wo=R.wo_s,
        g=R.g_s.at[:tokens],
        wd=R.wd_s,
        wg=R.wgu.at[:hidden],
        wu=R.wgu.at[hidden:],
    )

    def load(name):
        return pltpu.make_async_copy(getattr(R, name), spots[name], R.load_sem.at[LOADS.index(name)])

    for name in LOADS:
        load(name).start()

    barrier = pltpu.get_barrier_semaphore()

    def greet(axis, peer):
        pl.semaphore_signal(barrier, inc=1, device_id={axis: peer}, device_id_type=MESH_ID)

    for step in range(1, n_ctx):
        greet("context", lax.rem(ctx + step, n_ctx))
    for step in range(1, n_ten):
        greet("tensor", lax.rem(ten + step, n_ten))

    @pl.when(dp > 0)
    def _():
        greet("dp", dp - 1)

    @pl.when(dp < last)
    def _():
        greet("dp", dp + 1)

    load("x").wait()

    def norm_one():
        rows_in = R.x_s[...].astype(f32)
        scaled = rows_in * rms_scale(rows_in)
        return scaled, (scaled * R.gain1[...]).astype(bf16)

    n1f = norm_one()[1]
    for name in ("wq", "wk", "wv", "wgo"):
        load(name).wait()
    packed = mm(n1f, R.wcat[...])
    R.proj[:, :key_dim] = packed[:, :key_dim] * key_dim ** (-0.5)
    R.proj[:, key_dim:] = packed[:, key_dim:]
    expect = n_ctx + n_ten - 2

    @pl.when(jnp.logical_not(is_end))
    def _():
        pl.semaphore_wait(barrier, expect + 2)

    @pl.when(is_end)
    def _():
        pl.semaphore_wait(barrier, expect + 1)

    load("g").wait()
    R.sum_src[1] = R.g_s[:tokens, :].astype(f32).reshape(R.sum_src.shape[1:])

    def ext_copy(which, peer):
        if which == 0:
            src, dst = R.sum_src.at[1], R.shared.at[2]
        else:
            src, dst = R.shared.at[0, ten], R.shared.at[3, ten]
        return remote(src, dst, R.ext_sem.at[which, 0], R.ext_sem.at[which, 1], "dp", peer)

    @pl.when(is_end)
    def _():
        ext_copy(0, end_peer).start()

    low = mm_nt(n1f, R.wld[...])
    R.low[...] = low
    logits = hdot(low, R.wlu[...].astype(f32), ((1,), (0,))) + R.bias[...]
    R.logits[...] = logits
    R.rates[...] = (
        jnp.minimum(logits, 0.0) - jnp.log1p(jnp.exp(-jnp.abs(logits)))
    ) / GATE_NORM
    gla_states(R.proj, R.rates, R.cumuls, R.states, R.pair)

    def ctx_copy(which, src, slots, step):
        return remote(
            src,
            slots.at[step - 1],
            R.ctx_sem.at[which, 0, step - 1],
            R.ctx_sem.at[which, 1, step - 1],
            "context",
            lax.rem(ctx + step, n_ctx),
        )

    def fold(out_ref, slots, reverse):
        out_ref[...] = jnp.zeros_like(out_ref)
        for m in reversed(range(1, n_ctx)):
            index = n_ctx - m - 1 if reverse else m - 1

            @pl.when(ctx + m < n_ctx if reverse else ctx >= m)
            def _(index=index):
                out_ref[...] = (
                    slots[index, :, value_dim : value_dim + 1] * out_ref[...]
                    + slots[index, :, :value_dim]
                )

    for step in range(1, n_ctx):
        ctx_copy(0, R.pair, R.pair_slots, step).start()

    gla_outputs(R.proj, R.cumuls, R.states, R.o_s, R.decayed)
    for step in range(1, n_ctx):
        ctx_copy(0, R.pair, R.pair_slots, step).wait_recv()
    fold(R.entry, R.pair_slots, False)
    o = R.o_s[...] + hdot(R.decayed[...], R.entry[...], ((1,), (0,)))
    R.o_s[...] = o
    gate_in = R.proj[:, 2 * key_dim + value_dim :]
    scale_h = lax.rsqrt(jnp.mean(o * o, axis=-1, keepdims=True) + EPS_HEAD)
    gated = o * scale_h * R.hgain[...] * (gate_in * jax.nn.sigmoid(gate_in))
    load("wo").wait()

    def sum_copy(which, bank, n):
        src = R.sum_src
        source = (
            src.at[bank, far_ten, 0],
            src.at[bank, far_ten, 1],
            src.at[bank, near_ten, 0],
            src.at[bank, over_ten, 1],
            R.sum_via.at[bank, 0],
            R.sum_via.at[bank, 1],
        )[n]
        peer = (near_ten, over_ten, near_ten, over_ten, over_ten, near_ten)[n]
        return remote(
            source,
            R.sum_slots.at[bank, n],
            R.sum_sem.at[which, 0, n],
            R.sum_sem.at[which, 1, n],
            "tensor",
            peer,
        )

    def sum_start(which, bank, value=None):
        if value is not None:
            R.sum_src[bank] = value.reshape(n_ten, 2, own_rows // 2, model)
        for n in range(4):
            sum_copy(which, bank, n).start()

    def sum_relay(which, bank):
        sum_copy(which, bank, 0).wait_recv()
        R.sum_via[bank, 0] = R.sum_slots[bank, 0] + R.sum_src[bank, over_ten, 0]
        sum_copy(which, bank, 4).start()
        sum_copy(which, bank, 1).wait_recv()
        R.sum_via[bank, 1] = R.sum_slots[bank, 1] + R.sum_src[bank, near_ten, 1]
        sum_copy(which, bank, 5).start()

    def sum_end(which, bank):
        for n in range(2, 6):
            sum_copy(which, bank, n).wait_recv()
        slots = R.sum_slots
        own = R.sum_src
        return jnp.concatenate(
            [
                own[bank, ten, 0] + slots[bank, 2] + slots[bank, 4],
                own[bank, ten, 1] + slots[bank, 3] + slots[bank, 5],
            ],
            axis=0,
        )

    def sum_sent(which, bank):
        for n in range(6):
            sum_copy(which, bank, n).wait_send()

    def share_copy(which, n, arriving=False):
        if arriving:
            owner = (near_ten, over_ten, near_ten, over_ten, far_ten, far_ten)[n]
        else:
            owner = (ten, ten, ten, ten, near_ten, over_ten)[n]
        spot = R.shared.at[min(which, 3), owner, (0, 1, 1, 0, 0, 1)[n]]
        return remote(
            spot,
            spot,
            R.share_sem.at[which, 0, n],
            R.share_sem.at[which, 1, n],
            "tensor",
            (near_ten, over_ten, near_ten, over_ten, over_ten, near_ten)[n],
        )

    def share_start(which, value=None):
        if value is not None:
            R.shared[which, ten] = value.reshape(2, own_rows // 2, model)
        for n in range(4):
            share_copy(which, n).start()

    def share_relay(which):
        share_copy(which, 0, True).wait_recv()
        share_copy(which, 4).start()
        share_copy(which, 1, True).wait_recv()
        share_copy(which, 5).start()

    def share_end(which):
        for n in range(2, 6):
            share_copy(which, n, True).wait_recv()

    def share_sent(which):
        for n in range(6):
            share_copy(which, n).wait_send()

    arrays = len(pieces)
    cut = (1, 1, 0, 0, 0)
    heights = [R.made(i).shape[1] for i in range(arrays)]

    def rows(i, piece):
        height = heights[i] // pieces[i]
        return pl.ds(piece * height, height)

    def near_copy(i, step, dest, piece):
        peer = lax.rem(ctx + step, n_ctx)
        return remote(
            R.made(i).at[peer * n_dp + dest, rows(i, piece)],
            R.near(i).at[step - 1, dest, rows(i, piece)],
            R.near_sem(i).at[0, step - 1, dest, piece],
            R.near_sem(i).at[1, step - 1, dest, piece],
            "context",
            peer,
        )

    def line_copy(i, way, dest, piece, peer):
        goal = jnp.where(dest == peer, n_dp, dest) if way == 1 else dest
        return remote(
            R.line(i).at[dest, rows(i, piece)],
            R.line(i).at[goal, rows(i, piece)],
            R.line_sem(i).at[0, way, dest, piece],
            R.line_sem(i).at[1, way, dest, piece],
            "dp",
            peer,
        )

    def loop(low, high, body):
        if high - low == 1:
            body(low)
        else:

            def lap(index, carry):
                body(index)
                return carry

            lax.fori_loop(low, high, lap, 0)

    def over_pieces(i, body):
        loop(0, pieces[i], body)

    def over_steps(body):
        loop(1, n_ctx, body)

    def takes_part(i, dest):
        if not cut[i]:
            return True
        if dest == 0:
            return dp < last
        if dest == last:
            return dp > 0
        return jnp.logical_not(is_end)

    def guarded(condition, body):
        if condition is True:
            body()
        else:
            pl.when(condition)(body)

    def put(i, owner, dest):
        made = R.made(i)
        cols = pl.ds(pl.multiple_of(owner * part, part), part) if wide else None
        if i < 2:
            right = R.mixed if i == 0 else R.gpair
            left = R.g_s if i == 0 else R.n2_s
            both = jnp.logical_or(
                dp == 1 if dest >= 1 else False, dp == last - 1 if dest < last else False
            )

            @pl.when(both)
            def _():
                if wide:
                    made[owner] = mm(right[...], left[:, cols])
                else:
                    made[owner] = mm_nt(R.left(i)[owner], right[...])

            @pl.when(jnp.logical_not(both))
            def _():
                if wide:
                    made[owner] = mm(right[:, :tokens], left[:tokens, cols])
                else:
                    made[owner] = mm_nt(R.left(i)[owner, :, :tokens], right[:, :tokens])

        elif i == 2:
            if wide:
                made[owner] = mm(R.gated[...], R.n2_s[:tokens, cols])
            else:
                made[owner] = mm_nt(R.left0[owner, :, :tokens], R.gated[...])
        elif i == 3:
            made[owner] = mm(R.left3[owner], R.gproj[...])

    def make(i, dest):
        def body():
            def step_body(step):
                put(i, lax.rem(ctx + step, n_ctx) * n_dp + dest, dest)
                over_pieces(i, lambda piece: near_copy(i, step, dest, piece).start())

            over_steps(step_body)
            put(i, ctx * n_dp + dest, dest)

        guarded(takes_part(i, dest), body)

    def own_sum(i, dest, piece):
        total = R.made(i)[ctx * n_dp + dest, rows(i, piece)]
        for step in range(1, n_ctx):
            near_copy(i, step, dest, piece).wait_recv()
            total = total + R.near(i)[step - 1, dest, rows(i, piece)]
        return total

    def first_send(i, way, dest):
        start = cut[i] if way == 0 else last - cut[i]
        if dest <= start if way == 0 else dest >= start:
            return

        @pl.when(dp == start)
        def _():
            def body(piece):
                R.line(i)[dest, rows(i, piece)] = own_sum(i, dest, piece)
                line_copy(i, way, dest, piece, dp + 1 if way == 0 else dp - 1).start()

            over_pieces(i, body)

    def middle_send(i, way, dest, hop):
        reach = dest - cut[i] if way == 0 else last - cut[i] - dest
        if reach < (2 if hop == 1 else 3):
            return
        if way == 0:
            active = dp == cut[i] + 1
            if hop > 1:
                active = jnp.logical_and(dp > cut[i] + 1, dp < dest)
        else:
            active = dp == last - cut[i] - 1
            if hop > 1:
                active = jnp.logical_and(dp < last - cut[i] - 1, dp > dest)
        peer = dp + 1 if way == 0 else dp - 1

        @pl.when(active)
        def _():
            def body(piece):
                own = own_sum(i, dest, piece)
                line_copy(i, way, dest, piece, dp).wait_recv()
                R.line(i)[dest, rows(i, piece)] = (
                    R.line(i)[dest, rows(i, piece)] + own
                )
                line_copy(i, way, dest, piece, peer).start()

            over_pieces(i, body)

    def makes(i, k):
        for dest in dict.fromkeys((last - k, k)):
            make(i, dest)

    def firsts(i, k):
        first_send(i, 0, last - k)
        first_send(i, 1, k)

    def middles(i, k, hop):
        middle_send(i, 0, last - k, hop)
        middle_send(i, 1, k, hop)

    laps = -(-n_dp // 2)

    def build(i, begin=0):
        for k in range(begin, laps):
            makes(i, k)
            firsts(i, k)
        for k in range(laps, last):
            firsts(i, k)

    def finish(i, out):
        def body(piece):
            span = rows(i, piece)
            here = ctx * n_dp + dp
            made = R.made(i)
            made[here, span] = own_sum(i, dp, piece)

            @pl.when(dp > cut[i])
            def _():
                line_copy(i, 0, dp, piece, dp).wait_recv()
                made[here, span] += R.line(i)[dp, span]

            @pl.when(dp < last - cut[i])
            def _():
                line_copy(i, 1, dp, piece, dp).wait_recv()
                made[here, span] += R.line(i)[n_dp, span]

            out(span, made[here, span])

        over_pieces(i, body)

    def drain(i):
        for dest in range(n_dp):

            def near_sent(dest=dest):
                def body(piece):
                    for step in range(1, n_ctx):
                        near_copy(i, step, dest, piece).wait_send()

                over_pieces(i, body)

            guarded(takes_part(i, dest), near_sent)
            if dest > cut[i]:

                @pl.when(jnp.logical_and(dp >= cut[i], dp < dest))
                def _(dest=dest):
                    over_pieces(
                        i, lambda piece: line_copy(i, 0, dest, piece, dp + 1).wait_send()
                    )

            if dest < last - cut[i]:

                @pl.when(jnp.logical_and(dp <= last - cut[i], dp > dest))
                def _(dest=dest):
                    over_pieces(
                        i, lambda piece: line_copy(i, 1, dest, piece, dp - 1).wait_send()
                    )

    def turned(value):
        return value.T.reshape(owners, part, value.shape[0]).astype(bf16)

    sum_start(0, 0, mm(gated.astype(bf16), R.wo_s[...]))
    R.gated[...] = gated.T.astype(bf16)
    sum_relay(0, 0)
    R.left3[...] = turned(norm_one()[1].astype(f32))
    hid = R.x_s[mine, :].astype(f32) + sum_end(0, 0)
    R.hid[...] = hid
    gain2 = R.gain2[...]
    share_start(0, (hid * rms_scale(hid) * gain2).astype(bf16).astype(f32))

    @pl.when(is_end)
    def _():
        ext_copy(1, end_peer).start()

    load("wg").wait()
    load("wu").wait()
    load("wd").wait()
    sum_sent(0, 0)
    share_relay(0)
    R.gm[...] = mm_nt(R.wd_s[...], R.g_s[:tokens, :])

    @pl.when(absorbs)
    def _():
        ext_copy(0, absorb_peer).wait_recv()
        R.g_s[tokens:, :] = R.shared[2].reshape(tokens, model).astype(bf16)
        ext_copy(1, absorb_peer).wait_recv()
        share_start(4)

    share_end(0)

    def feed_forward(half):
        span = slice(half * tokens, (half + 1) * tokens)
        n2 = R.n2_s[span, :]
        ffn_gate = mm_nt(R.wgu[:hidden, :], n2)
        ffn_up = mm_nt(R.wgu[hidden:, :], n2)
        R.mixed[:, span] = (ffn_gate * jax.nn.sigmoid(ffn_gate) * ffn_up).astype(bf16)
        R.ffn_gate[...] = ffn_gate
        R.ffn_up[...] = ffn_up

    def feed_back(half):
        span = slice(half * tokens, (half + 1) * tokens)
        grad_mixed, ffn_gate, ffn_up = R.gm[...], R.ffn_gate[...], R.ffn_up[...]
        sig = jax.nn.sigmoid(ffn_gate)
        R.gpair[:hidden, span] = (
            grad_mixed * ffn_up * (sig * (1.0 + ffn_gate * (1.0 - sig)))
        ).astype(bf16)
        R.gpair[hidden:, span] = (grad_mixed * (ffn_gate * sig)).astype(bf16)

    R.n2_s[:tokens, :] = R.shared[0].reshape(tokens, model).astype(bf16)
    feed_forward(0)
    feed_back(0)

    @pl.when(absorbs)
    def _():
        share_relay(4)
        R.gm[...] = mm_nt(R.wd_s[...], R.g_s[tokens:, :])

    ffn_part = mm_tn(R.gpair[:, :tokens], R.wgu[...])
    R.sum_src[0] = ffn_part.reshape(R.sum_src.shape[1:])

    @pl.when(absorbs)
    def _():
        share_end(4)

    sum_start(1, 0)

    @pl.when(absorbs)
    def _():
        R.n2_s[tokens:, :] = R.shared[3].reshape(tokens, model).astype(bf16)
        feed_forward(1)

    if not wide:
        for at in range(0, 2 * tokens, 128):
            span = slice(at, at + 128)
            R.left0[:, :, span] = turned(R.g_s[span, :].astype(f32))
            R.left1[:, :, span] = turned(R.n2_s[span, :].astype(f32))
    makes(0, 0)
    sum_relay(1, 0)
    firsts(0, 0)

    @pl.when(absorbs)
    def _():
        feed_back(1)

    grad_normed_two = sum_end(1, 0)
    hid = R.hid[...]
    grad_two_rows, gain_two_part = norm_back(hid, rms_scale(hid), gain2, grad_normed_two)
    grad_hidden = R.g_s[mine, :].astype(f32) + grad_two_rows
    R.gh[...] = grad_hidden
    share_start(1, grad_hidden.astype(bf16).astype(f32))
    sum_sent(1, 0)
    build(0, 1)
    share_relay(1)

    @pl.when(is_end)
    def _():
        ext_copy(0, end_peer).wait_send()

    sum_start(2, 1, mm_tn(R.mixed[:, :tokens], R.wd_s[...]))
    build(1)
    middles(0, 0, 1)
    share_end(1)

    R.n2_s[:tokens, :] = R.shared[1].reshape(tokens, model).astype(bf16)
    grad_gated = mm_nt(R.n2_s[:tokens, :], R.wo_s[...])
    o = R.o_s[...]
    gate_in = R.proj[:, 2 * key_dim + value_dim :]
    scale_h = lax.rsqrt(jnp.mean(o * o, axis=-1, keepdims=True) + EPS_HEAD)
    sig = jax.nn.sigmoid(gate_in)
    soft = gate_in * sig
    hgain = R.hgain[...]
    normal = o * scale_h
    head_part = jnp.sum(grad_gated * normal * soft, axis=0, keepdims=True)
    R.gproj[:, 2 * key_dim + value_dim :] = (
        grad_gated * normal * hgain * (sig * (1.0 + gate_in * (1.0 - sig)))
    ).astype(bf16)
    back = grad_gated * hgain * soft
    go = scale_h * (
        back - normal * scale_h * jnp.mean(back * o, axis=-1, keepdims=True)
    )
    R.go[...] = go
    R.pair_back[:, :value_dim] = hdot(R.decayed[...], go, ((0,), (0,)))
    R.pair_back[:, value_dim:] = R.pair[:, value_dim:]
    for step in range(1, n_ctx):
        ctx_copy(1, R.pair_back, R.back_slots, step).start()
    sum_relay(2, 1)
    if not wide:
        R.left0[:, :, :tokens] = turned(R.shared[1].reshape(tokens, model))
    build(2)
    for step in range(1, n_ctx):
        ctx_copy(1, R.pair_back, R.back_slots, step).wait_recv()
    fold(R.later, R.back_slots, True)
    gla_backward(
        R.proj, R.cumuls, R.states, R.entry, R.later, R.go, R.gproj, R.dr
    )
    grad_logits = R.dr[...] * jax.nn.sigmoid(-R.logits[...]) / GATE_NORM
    grad_low = hdot(grad_logits, R.wlu[...].astype(f32), ((1,), (1,)))

    @pl.when(absorbs)
    def _():
        share_sent(4)

    sum_start(
        3,
        0,
        mm_nt(R.gproj[...], R.wcat[...])
        + hdot(grad_low, R.wld[...].astype(f32), ((1,), (0,))),
    )
    scaled, n1f = norm_one()
    low_down = hdot(grad_low, n1f.astype(f32), ((0,), (0,)))
    low_up = hdot(R.low[...], grad_logits, ((0,), (0,)))
    bias_part = jnp.sum(grad_logits, axis=0, keepdims=True)
    gain_one_part = jnp.sum(
        R.sum_src[0].reshape(tokens, model) * scaled, axis=0, keepdims=True
    )
    R.made4[...] = jnp.zeros_like(R.made4)
    part_head = value_dim // owners
    part_key = key_dim // owners
    tail = R.tail_slots.shape[1]
    for owner in range(owners):
        span = slice(owner * part, (owner + 1) * part)
        R.made4[owner, :rank, :part] = low_down[:, span]
        R.made4[owner, rank : rank + 1, :part] = gain_one_part[:, span]
        R.made4[owner, rank + 1 : rank + 2, :part] = gain_two_part[:, span]
        R.made4[owner, rank + 2 : rank + 3, :part_head] = head_part[
            :, owner * part_head : (owner + 1) * part_head
        ]
        span = slice(owner * part_key, (owner + 1) * part_key)
        R.made4[owner, tail : tail + rank, :part_key] = low_up[:, span]
        R.made4[owner, tail + rank : tail + rank + 1, :part_key] = bias_part[:, span]
    build(4)
    build(3)
    sum_relay(3, 0)
    for k in range(last):
        middles(2, k, 1)
    for k in range(last):
        middles(4, k, 1)
    middles(1, 0, 1)
    result = R.hid[...] + sum_end(2, 1)
    share_start(2, result.astype(bf16).astype(f32))
    middles(3, 0, 1)
    grad_normed_one = sum_end(3, 0)
    own_in = R.x_s[mine, :].astype(f32)
    grad_one_rows, _ = norm_back(own_in, rms_scale(own_in), R.gain1[...], grad_normed_one)
    share_relay(2)
    share_start(3, R.gh[...] + grad_one_rows)
    for i in range(2):
        for k in range(1, last):
            middles(i, k, 1)
    for k in range(1, last):
        middles(3, k, 1)
    share_relay(3)
    for i in (0, 1, 2, 4, 3):
        for k in range(last):
            middles(i, k, 2)

    def into(name):
        def out(span, value):
            getattr(R, name)[span, :] = value

        return out

    def put_proj(span, value):
        R.gq[span, :] = value[:, :key_dim]
        R.gk[span, :] = value[:, key_dim : 2 * key_dim]
        R.gv[span, :] = value[:, 2 * key_dim : 2 * key_dim + value_dim]
        R.ggo[span, :] = value[:, 2 * key_dim + value_dim :]

    finish(0, into("gdown"))
    finish(1, into("gpairs"))
    share_end(2)
    R.result[...] = R.shared[2].reshape(tokens, model).astype(bf16)
    finish(2, into("gout"))
    finish(4, into("pack"))
    R.tail_slots[ten] = R.pack[:tail, :]

    def tail_copy(sender, peer, step):
        spot = R.tail_slots.at[sender]
        return remote(
            spot, spot, R.tail_sem.at[0, step - 1], R.tail_sem.at[1, step - 1], "tensor", peer
        )

    for step in range(1, n_ten):
        tail_copy(ten, lax.rem(ten + step, n_ten), step).start()
    finish(3, put_proj)
    share_end(3)
    R.gin[...] = R.shared[3].reshape(tokens, model)
    for step in range(1, n_ten):
        sender = lax.rem(ten + n_ten - step, n_ten)
        tail_copy(sender, sender, step).wait_recv()
    total = R.tail_slots[0]
    for index in range(1, n_ten):
        total = total + R.tail_slots[index]
    R.pack[:tail, :] = total

    for step in range(1, n_ctx):
        ctx_copy(0, R.pair, R.pair_slots, step).wait_send()
        ctx_copy(1, R.pair_back, R.back_slots, step).wait_send()
    sum_sent(2, 1)
    sum_sent(3, 0)
    for which in range(4):
        share_sent(which)

    @pl.when(is_end)
    def _():
        ext_copy(1, end_peer).wait_send()

    for i in range(arrays):
        drain(i)
    for step in range(1, n_ten):
        tail_copy(ten, lax.rem(ten + step, n_ten), step).wait_send()


def hand_out_kernel(moves, n_in, n_big, *refs):
    ins, pack_ref = refs[: n_in - 1], refs[n_in - 1]
    big = refs[n_in : n_in + n_big]
    small = refs[n_in + n_big : -1]
    sems = refs[-1]
    copies = []
    for at, (source, first, rows) in enumerate(moves):
        src = ins[source] if rows is None else ins[source].at[first : first + rows]
        copies.append(pltpu.make_async_copy(src, big[at], sems.at[at]))
        copies[-1].start()
    low_down, gain1, gain2, hgain, low_up, bias = small
    rank, part = low_down.shape
    tail = -(-(rank + 3) // 8) * 8
    low_down[...] = pack_ref[:rank, :part]
    gain1[...] = pack_ref[rank : rank + 1, :part]
    gain2[...] = pack_ref[rank + 1 : rank + 2, :part]
    hgain[...] = pack_ref[rank + 2 : rank + 3, : hgain.shape[1]]
    low_up[...] = pack_ref[tail : tail + rank, : low_up.shape[1]]
    bias[...] = pack_ref[tail + rank : tail + rank + 1, : bias.shape[1]]
    for copy in copies:
        copy.wait()


def shards(
    inputs,
    norm_gain1,
    w_query,
    w_key,
    w_value,
    w_gate_out,
    w_low_down,
    w_low_up,
    forget_bias,
    head_gain,
    w_output,
    norm_gain2,
    w_ffn_gate,
    w_ffn_up,
    w_ffn_down,
    cotangent,
):
    bf16, f32 = jnp.bfloat16, jnp.float32
    n_ctx, n_dp, n_ten = (lax.axis_size(axis) for axis in ("context", "dp", "tensor"))
    owners = n_ctx * n_dp
    model = inputs.shape[-1]
    x = inputs.reshape(-1, model)
    tokens = x.shape[0]
    key_dim, value_dim, hidden = w_query.shape[1], w_value.shape[1], w_ffn_gate.shape[1]
    assert inputs.shape[0] == 1 and head_gain.shape[0] == value_dim
    assert n_ten == 4 and n_dp >= 4
    rank = w_low_down.shape[1]
    part = model // owners
    wide = part % 128 == 0
    own_rows = tokens // n_ten
    width = 2 * key_dim + 2 * value_dim
    tail = -(-(rank + 3) // 8) * 8
    pack_rows = tail + -(-(rank + 1) // 8) * 8

    ins = dict(
        x=x,
        gain1=norm_gain1[None],
        wq=w_query,
        wk=w_key,
        wv=w_value,
        wgo=w_gate_out,
        wld=w_low_down.T,
        wlu=w_low_up,
        bias=forget_bias[None],
        hgain=head_gain[None],
        wo=w_output,
        gain2=norm_gain2[None],
        wg=w_ffn_gate.T,
        wu=w_ffn_up.T,
        wd=w_ffn_down,
        g=cotangent.reshape(-1, model),
    )

    def owned(extent):
        return (extent, part) if wide else (part, extent)

    shapes = [owned(hidden), owned(2 * hidden), owned(value_dim), (part, width), (pack_rows, 128)]
    outs = dict(
        result=((tokens, model), bf16),
        gin=((tokens, model), f32),
        gq=((part, key_dim), f32),
        gk=((part, key_dim), f32),
        gv=((part, value_dim), f32),
        ggo=((part, value_dim), f32),
        gout=(shapes[2], f32),
        gpairs=(shapes[1], f32),
        gdown=(shapes[0], f32),
        pack=((pack_rows, 128), f32),
    )
    pieces = []
    for shape in shapes:
        count = 4
        while shape[0] % (count * 8):
            count //= 2
        pieces.append(count if shape[0] * shape[1] > 16384 else 1)

    dma = pltpu.SemaphoreType.DMA
    scratch = dict(
        x_s=pltpu.VMEM((tokens, model), bf16),
        g_s=pltpu.VMEM((2 * tokens, model), bf16),
        ext_sem=dma((2, 2)),
        wcat=pltpu.VMEM((model, width), bf16),
        wo_s=pltpu.VMEM((value_dim, model), bf16),
        wgu=pltpu.VMEM((2 * hidden, model), bf16),
        wd_s=pltpu.VMEM((hidden, model), bf16),
        load_sem=dma((len(LOADS),)),
        n2_s=pltpu.VMEM((2 * tokens, model), bf16),
        proj=pltpu.VMEM((tokens, width), f32),
        low=pltpu.VMEM((tokens, rank), f32),
        logits=pltpu.VMEM((tokens, key_dim), f32),
        rates=pltpu.VMEM((tokens, key_dim), f32),
        cumuls=pltpu.VMEM((tokens, key_dim), f32),
        o_s=pltpu.VMEM((tokens, value_dim), f32),
        decayed=pltpu.VMEM((tokens, key_dim), f32),
        states=pltpu.VMEM((tokens // BLOCK, key_dim, value_dim), f32),
        pair=pltpu.VMEM((key_dim, value_dim + key_dim), f32),
        pair_back=pltpu.VMEM((key_dim, value_dim + key_dim), f32),
        pair_slots=pltpu.VMEM((n_ctx - 1, key_dim, value_dim + key_dim), f32),
        back_slots=pltpu.VMEM((n_ctx - 1, key_dim, value_dim + key_dim), f32),
        ctx_sem=dma((2, 2, n_ctx - 1)),
        entry=pltpu.VMEM((key_dim, value_dim), f32),
        later=pltpu.VMEM((key_dim, value_dim), f32),
        gm=pltpu.VMEM((hidden, tokens), f32),
        ffn_gate=pltpu.VMEM((hidden, tokens), f32),
        ffn_up=pltpu.VMEM((hidden, tokens), f32),
        gated=pltpu.VMEM((value_dim, tokens), bf16),
        sum_src=pltpu.VMEM((2, n_ten, 2, own_rows // 2, model), f32),
        sum_slots=pltpu.VMEM((2, 6, own_rows // 2, model), f32),
        sum_via=pltpu.VMEM((2, 2, own_rows // 2, model), f32),
        sum_sem=dma((4, 2, 6)),
        shared=pltpu.VMEM((4, n_ten, 2, own_rows // 2, model), f32),
        share_sem=dma((5, 2, 6)),
        hid=pltpu.VMEM((own_rows, model), f32),
        gh=pltpu.VMEM((own_rows, model), f32),
        mixed=pltpu.VMEM((hidden, 2 * tokens), bf16),
        gpair=pltpu.VMEM((2 * hidden, 2 * tokens), bf16),
        go=pltpu.VMEM((tokens, value_dim), f32),
        dr=pltpu.VMEM((tokens, key_dim), f32),
        gproj=pltpu.VMEM((tokens, width), bf16),
        tail_slots=pltpu.VMEM((n_ten, tail, 128), f32),
        tail_sem=dma((2, n_ten - 1)),
        left3=pltpu.VMEM((owners, part, tokens), bf16),
    )
    if not wide:
        scratch["left0"] = pltpu.VMEM((owners, part, 2 * tokens), bf16)
        scratch["left1"] = pltpu.VMEM((owners, part, 2 * tokens), bf16)
    for i, shape in enumerate(shapes):
        scratch["made%d" % i] = pltpu.VMEM((owners,) + shape, f32)
        scratch["near%d" % i] = pltpu.VMEM((n_ctx - 1, n_dp) + shape, f32)
        scratch["line%d" % i] = pltpu.VMEM((n_dp + 1,) + shape, f32)
        scratch["near_sem%d" % i] = dma((2, n_ctx - 1, n_dp, pieces[i]))
        scratch["line_sem%d" % i] = dma((2, 2, n_dp, pieces[i]))

    names = tuple(ins) + tuple(outs) + tuple(scratch)
    made = pl.pallas_call(
        functools.partial(block_kernel, (n_ctx, n_dp, n_ten), names, tuple(pieces), wide),
        out_shape=tuple(jax.ShapeDtypeStruct(shape, kind) for shape, kind in outs.values()),
        in_specs=[
            pl.BlockSpec(memory_space=pl.ANY if name in LOADS else VMEM) for name in ins
        ],
        out_specs=tuple([pl.BlockSpec(memory_space=VMEM)] * len(outs)),
        scratch_shapes=list(scratch.values()),
        compiler_params=pltpu.CompilerParams(
            collective_id=0, has_side_effects=True, vmem_limit_bytes=VMEM_LIMIT
        ),
        name="gla_block",
    )(*ins.values())
    part_head = value_dim // owners
    part_key = key_dim // owners
    moves, big_shapes = [], []
    for at, name in enumerate(list(outs)[:-1]):
        shape, kind = outs[name]
        if name == "gpairs" and wide:
            for half in range(2):
                moves.append((at, half * hidden, hidden))
                big_shapes.append(((hidden, part), kind))
        else:
            moves.append((at, 0, None))
            big_shapes.append((shape, kind))
    small_shapes = [
        (rank, part),
        (1, part),
        (1, part),
        (1, part_head),
        (rank, part_key),
        (1, part_key),
    ]
    done = pl.pallas_call(
        functools.partial(hand_out_kernel, tuple(moves), len(made), len(moves)),
        out_shape=tuple(
            [jax.ShapeDtypeStruct(shape, kind) for shape, kind in big_shapes]
            + [jax.ShapeDtypeStruct(shape, f32) for shape in small_shapes]
        ),
        in_specs=[pl.BlockSpec(memory_space=VMEM)] * len(made),
        out_specs=tuple(
            [pl.BlockSpec(memory_space=pl.ANY)] * len(moves)
            + [pl.BlockSpec(memory_space=VMEM)] * len(small_shapes)
        ),
        scratch_shapes=[dma((len(moves),))],
        name="hand_out",
    )(*made)
    low_down, gain1, gain2, hgain, low_up, bias = done[len(moves) :]
    result, gin, gq, gk, gv, ggo, gout = done[:7]
    if wide:
        ggate, gup, gdown = done[7].T, done[8].T, done[9]
    else:
        ggate, gup = done[7][:, :hidden], done[7][:, hidden:]
        gdown, gout = done[8].T, gout.T
    return (
        result.reshape(inputs.shape),
        gin.reshape(inputs.shape),
        gain1.reshape(-1),
        gq,
        gk,
        gv,
        ggo,
        low_down.T,
        low_up,
        bias.reshape(-1),
        hgain.reshape(-1),
        gout,
        gain2.reshape(-1),
        ggate,
        gup,
        gdown,
    )


def solution(mesh):
    return jax.shard_map(
        shards,
        mesh=mesh,
        in_specs=(
            P("dp", "context", None),
            P(),
            P(None, "tensor"),
            P(None, "tensor"),
            P(None, "tensor"),
            P(None, "tensor"),
            P(),
            P(None, "tensor"),
            P("tensor"),
            P(),
            P("tensor", None),
            P(),
            P(None, "tensor"),
            P(None, "tensor"),
            P("tensor", None),
            P("dp", "context", None),
        ),
        out_specs=(
            P("dp", "context", None),
            P("dp", "context", None),
            P(("context", "dp")),
            P(("context", "dp"), "tensor"),
            P(("context", "dp"), "tensor"),
            P(("context", "dp"), "tensor"),
            P(("context", "dp"), "tensor"),
            P(("context", "dp"), None),
            P(None, ("tensor", "context", "dp")),
            P(("tensor", "context", "dp")),
            P(("context", "dp")),
            P("tensor", ("context", "dp")),
            P(("context", "dp")),
            P(("context", "dp"), "tensor"),
            P(("context", "dp"), "tensor"),
            P("tensor", ("context", "dp")),
        ),
        check_vma=False,
    )
```

```python
import functools

import jax
import jax.numpy as jnp
from jax import lax
from jax.experimental import pallas as pl
from jax.experimental.pallas import tpu as pltpu
from jax.sharding import PartitionSpec as P

BLOCK = 64


EPS_MODEL = 1e-06
EPS_HEAD = 1e-05
GATE_NORM = 16.0
HIGHEST = lax.Precision.HIGHEST


VMEM_LIMIT = 63 * 1024 * 1024
VMEM = pltpu.MemorySpace.VMEM
MESH_ID = pl.DeviceIdType.MESH


def hdot(left, right, dims):
    return lax.dot_general(
        left, right, (dims, ((), ())), precision=HIGHEST, preferred_element_type=jnp.float32
    )


def hdot3(left, right, dims):
    f32, bf16 = jnp.float32, jnp.bfloat16

    def halves(value):
        high = value.astype(bf16)
        return high, (value - high.astype(f32)).astype(bf16)

    def dot(one, two):
        return lax.dot_general(one, two, (dims, ((), ())), preferred_element_type=f32)

    (left_high, left_low), (right_high, right_low) = halves(left), halves(right)
    return dot(left_high, right_high) + (dot(left_high, right_low) + dot(left_low, right_high))


def mm(left, right):
    return jnp.dot(left, right, preferred_element_type=jnp.float32)


def mm_nt(left, right):
    return lax.dot_general(
        left, right, (((1,), (1,)), ((), ())), preferred_element_type=jnp.float32
    )


def column_of(row, height):
    return jnp.broadcast_to(row, (height, row.shape[1])).T


def triangle(length):
    rows = lax.broadcasted_iota(jnp.int32, (length, length), 0)
    cols = lax.broadcasted_iota(jnp.int32, (length, length), 1)
    return rows >= cols


def rms_scale(rows_in):
    return lax.rsqrt(jnp.mean(rows_in * rows_in, axis=-1, keepdims=True) + EPS_MODEL)


def norm_back(rows_in, scale_rows, gain_in, grad_normed):
    weighted = gain_in * grad_normed
    grad_gain = jnp.sum(grad_normed * rows_in * scale_rows, axis=0, keepdims=True)
    grad_rows = scale_rows * (
        weighted
        - rows_in * scale_rows * scale_rows * jnp.mean(weighted * rows_in, axis=-1, keepdims=True)
    )
    return (grad_rows, grad_gain)


def gla_states(proj, rates, cumuls_ref, states_ref, pair_ref):
    tokens, key_dim = rates.shape
    value_dim = states_ref.shape[2]
    ones_low = triangle(BLOCK).astype(jnp.float32)
    state = jnp.zeros((key_dim, value_dim), jnp.float32)
    before = jnp.zeros((1, key_dim), jnp.float32)
    for block in range(tokens // BLOCK):
        span = pl.ds(block * BLOCK, BLOCK)
        keys_in = proj[span, key_dim : 2 * key_dim]
        values_in = proj[span, 2 * key_dim : 2 * key_dim + value_dim]
        cumul = hdot(ones_low, rates[span, :], ((1,), (0,)))
        cumuls_ref[span, :] = cumul
        end_log = cumul[BLOCK - 1 :, :]
        states_ref[block] = state
        added = hdot3(keys_in * jnp.exp(end_log - cumul), values_in, ((0,), (0,)))
        state = column_of(jnp.exp(end_log), key_dim)[:, :1] * state + added
        before = before + end_log
    pair_ref[:, :value_dim] = state
    pair_ref[:, value_dim:] = column_of(jnp.exp(before), key_dim)


def gla_outputs(proj, cumuls_ref, states_ref, out_ref, decayed_ref):
    tokens, key_dim = cumuls_ref.shape
    value_dim = states_ref.shape[2]
    causal = triangle(BLOCK)
    before = jnp.zeros((1, key_dim), jnp.float32)
    for block in range(tokens // BLOCK):
        span = pl.ds(block * BLOCK, BLOCK)
        queries = proj[span, :key_dim]
        keys_in = proj[span, key_dim : 2 * key_dim]
        values_in = proj[span, 2 * key_dim : 2 * key_dim + value_dim]
        cumul = cumuls_ref[span, :]
        end_log = cumul[BLOCK - 1 :, :]
        anchor = 0.5 * end_log
        scores = hdot3(
            queries * jnp.exp(cumul - anchor), keys_in * jnp.exp(anchor - cumul), ((1,), (1,))
        )
        scores = jnp.where(causal, scores, 0.0)
        out_ref[span, :] = hdot3(scores, values_in, ((1,), (0,))) + hdot3(
            queries * jnp.exp(cumul), states_ref[block], ((1,), (0,))
        )
        decayed_ref[span, :] = queries * jnp.exp(cumul + before)
        before = before + end_log


def gla_backward(proj, cumuls_ref, states_ref, entry_ref, later_ref, g_ref, dqkv_ref, dr_ref):
    tokens, key_dim = cumuls_ref.shape
    value_dim = g_ref.shape[1]
    causal = triangle(BLOCK)
    ones_low = causal.astype(jnp.float32)
    blocks = tokens // BLOCK
    cumuls, befores = [], []
    before = jnp.zeros((1, key_dim), jnp.float32)
    for block in range(blocks):
        cumul = cumuls_ref[pl.ds(block * BLOCK, BLOCK), :]
        cumuls.append(cumul)
        befores.append(before)
        before = before + cumul[BLOCK - 1 :, :]
    grad_state = later_ref[...]
    entry = entry_ref[...]
    for block in reversed(range(blocks)):
        span = pl.ds(block * BLOCK, BLOCK)
        queries = proj[span, :key_dim]
        keys_in = proj[span, key_dim : 2 * key_dim]
        values_in = proj[span, 2 * key_dim : 2 * key_dim + value_dim]
        grad_out = g_ref[span, :]
        cumul = cumuls[block]
        end_log = cumul[BLOCK - 1 :, :]
        anchor = 0.5 * end_log
        state = states_ref[block] + column_of(jnp.exp(befores[block]), key_dim)[:, :1] * entry
        up, down = jnp.exp(cumul - anchor), jnp.exp(anchor - cumul)
        grow, rest = jnp.exp(cumul), jnp.exp(end_log - cumul)
        q_up, k_down = queries * up, keys_in * down
        scores = jnp.where(causal, hdot(q_up, k_down, ((1,), (1,))), 0.0)
        grad_scores = jnp.where(causal, hdot(grad_out, values_in, ((1,), (1,))), 0.0)
        grad_q = hdot(grad_scores, k_down, ((1,), (0,))) * up + grow * hdot(
            grad_out, state, ((1,), (1,))
        )
        carried_k = hdot(values_in, grad_state, ((1,), (1,))) * rest
        grad_k = hdot(grad_scores, q_up, ((0,), (0,))) * down + carried_k
        dqkv_ref[span, 2 * key_dim : 2 * key_dim + value_dim] = (
            hdot(scores, grad_out, ((0,), (0,)))
            + hdot(keys_in * rest, grad_state, ((1,), (0,)))
        ).astype(dqkv_ref.dtype)
        dqkv_ref[span, :key_dim] = (grad_q * key_dim ** (-0.5)).astype(dqkv_ref.dtype)
        dqkv_ref[span, key_dim : 2 * key_dim] = grad_k.astype(dqkv_ref.dtype)
        grad_cumul = queries * grad_q - keys_in * grad_k
        end_column = column_of(jnp.exp(end_log), key_dim)
        state_term = jnp.sum(grad_state * state, axis=1, keepdims=True) * end_column
        grad_end = state_term.T[:1, :] + jnp.sum(carried_k * keys_in, axis=0, keepdims=True)
        dr_ref[span, :] = hdot(ones_low, grad_cumul, ((0,), (0,))) + grad_end
        grad_state = end_column[:, :1] * grad_state + hdot(
            queries * grow, grad_out, ((0,), (0,))
        )


LEAVES = ("result", "gin", "gq", "gk", "gv", "ggo", "gout", "gpairs", "gdown", "pack")
LOADS = ("x", "wq", "wk", "wv", "wgo", "wo", "g", "wd", "wg", "wu")


class Refs:
    def __init__(self, pairs):
        self.__dict__.update(pairs)

    def made(self, i):
        return getattr(self, "made%d" % i)

    def near(self, i):
        return getattr(self, "near%d" % i)

    def line(self, i):
        return getattr(self, "line%d" % i)

    def near_sem(self, i):
        return getattr(self, "near_sem%d" % i)

    def line_sem(self, i):
        return getattr(self, "line_sem%d" % i)

    def left(self, i):
        return getattr(self, "left%d" % i)


def mm_tn(left, right):
    return lax.dot_general(
        left, right, (((0,), (0,)), ((), ())), preferred_element_type=jnp.float32
    )


def block_kernel(sizes, names, pieces, wide, *refs):
    f32, bf16 = jnp.float32, jnp.bfloat16
    n_ctx, n_dp, n_ten = sizes
    R = Refs(zip(names, refs))
    ctx = lax.axis_index("context")
    dp = lax.axis_index("dp")
    ten = lax.axis_index("tensor")
    tokens, model = R.x_s.shape
    key_dim = R.wq.shape[1]
    value_dim = R.wv.shape[1]
    hidden = R.wg.shape[0]
    rank = R.wld.shape[0]
    own_rows = tokens // n_ten
    owners = n_ctx * n_dp
    part = model // owners
    last = n_dp - 1
    mine = pl.ds(pl.multiple_of(ten * own_rows, own_rows), own_rows)
    near_ten = ten + 1 - 2 * lax.rem(ten, 2)
    over_ten = lax.rem(ten + 2, 4)
    far_ten = lax.rem(near_ten + 2, 4)
    is_end = jnp.logical_or(dp == 0, dp == last)
    absorbs = jnp.logical_or(dp == 1, dp == last - 1)
    end_peer = jnp.where(dp == 0, 1, last - 1)
    absorb_peer = jnp.where(dp == 1, 0, last)

    def remote(src, dst, send, recv, axis, peer):
        return pltpu.make_async_remote_copy(
            src_ref=src,
            dst_ref=dst,
            send_sem=send,
            recv_sem=recv,
            device_id={axis: peer},
            device_id_type=MESH_ID,
        )

    spots = dict(
        x=R.x_s,
        wq=R.wcat.at[:, :key_dim],
        wk=R.wcat.at[:, key_dim : 2 * key_dim],
        wv=R.wcat.at[:, 2 * key_dim : 2 * key_dim + value_dim],
        wgo=R.wcat.at[:, 2 * key_dim + value_dim :],
        wo=R.wo_s,
        g=R.g_s.at[:tokens],
        wd=R.wd_s,
        wg=R.wgu.at[:hidden],
        wu=R.wgu.at[hidden:],
    )

    def load(name):
        return pltpu.make_async_copy(getattr(R, name), spots[name], R.load_sem.at[LOADS.index(name)])

    for name in LOADS:
        load(name).start()

    barrier = pltpu.get_barrier_semaphore()

    def greet(axis, peer):
        pl.semaphore_signal(barrier, inc=1, device_id={axis: peer}, device_id_type=MESH_ID)

    for step in range(1, n_ctx):
        greet("context", lax.rem(ctx + step, n_ctx))
    for step in range(1, n_ten):
        greet("tensor", lax.rem(ten + step, n_ten))

    @pl.when(dp > 0)
    def _():
        greet("dp", dp - 1)

    @pl.when(dp < last)
    def _():
        greet("dp", dp + 1)

    load("x").wait()

    def norm_one():
        rows_in = R.x_s[...].astype(f32)
        scaled = rows_in * rms_scale(rows_in)
        return scaled, (scaled * R.gain1[...]).astype(bf16)

    n1f = norm_one()[1]
    for name in ("wq", "wk", "wv", "wgo"):
        load(name).wait()
    packed = mm(n1f, R.wcat[...])
    R.proj[:, :key_dim] = packed[:, :key_dim] * key_dim ** (-0.5)
    R.proj[:, key_dim:] = packed[:, key_dim:]
    expect = n_ctx + n_ten - 2

    @pl.when(jnp.logical_not(is_end))
    def _():
        pl.semaphore_wait(barrier, expect + 2)

    @pl.when(is_end)
    def _():
        pl.semaphore_wait(barrier, expect + 1)

    load("g").wait()
    R.sum_src[1] = R.g_s[:tokens, :].astype(f32).reshape(R.sum_src.shape[1:])

    def ext_copy(which, peer):
        if which == 0:
            src, dst = R.sum_src.at[1], R.shared.at[2]
        else:
            src, dst = R.shared.at[0, ten], R.shared.at[3, ten]
        return remote(src, dst, R.ext_sem.at[which, 0], R.ext_sem.at[which, 1], "dp", peer)

    @pl.when(is_end)
    def _():
        ext_copy(0, end_peer).start()

    low = mm_nt(n1f, R.wld[...])
    R.low[...] = low
    logits = hdot(low, R.wlu[...].astype(f32), ((1,), (0,))) + R.bias[...]
    R.logits[...] = logits
    R.rates[...] = (
        jnp.minimum(logits, 0.0) - jnp.log1p(jnp.exp(-jnp.abs(logits)))
    ) / GATE_NORM
    gla_states(R.proj, R.rates, R.cumuls, R.states, R.pair)

    def ctx_copy(which, src, slots, step):
        return remote(
            src,
            slots.at[step - 1],
            R.ctx_sem.at[which, 0, step - 1],
            R.ctx_sem.at[which, 1, step - 1],
            "context",
            lax.rem(ctx + step, n_ctx),
        )

    def fold(out_ref, slots, reverse):
        out_ref[...] = jnp.zeros_like(out_ref)
        for m in reversed(range(1, n_ctx)):
            index = n_ctx - m - 1 if reverse else m - 1

            @pl.when(ctx + m < n_ctx if reverse else ctx >= m)
            def _(index=index):
                out_ref[...] = (
                    slots[index, :, value_dim : value_dim + 1] * out_ref[...]
                    + slots[index, :, :value_dim]
                )

    for step in range(1, n_ctx):
        ctx_copy(0, R.pair, R.pair_slots, step).start()

    gla_outputs(R.proj, R.cumuls, R.states, R.o_s, R.decayed)
    for step in range(1, n_ctx):
        ctx_copy(0, R.pair, R.pair_slots, step).wait_recv()
    fold(R.entry, R.pair_slots, False)
    o = R.o_s[...] + hdot(R.decayed[...], R.entry[...], ((1,), (0,)))
    R.o_s[...] = o
    gate_in = R.proj[:, 2 * key_dim + value_dim :]
    scale_h = lax.rsqrt(jnp.mean(o * o, axis=-1, keepdims=True) + EPS_HEAD)
    gated = o * scale_h * R.hgain[...] * (gate_in * jax.nn.sigmoid(gate_in))
    load("wo").wait()

    def sum_copy(which, bank, n):
        src = R.sum_src
        source = (
            src.at[bank, far_ten, 0],
            src.at[bank, far_ten, 1],
            src.at[bank, near_ten, 0],
            src.at[bank, over_ten, 1],
            R.sum_via.at[bank, 0],
            R.sum_via.at[bank, 1],
        )[n]
        peer = (near_ten, over_ten, near_ten, over_ten, over_ten, near_ten)[n]
        return remote(
            source,
            R.sum_slots.at[bank, n],
            R.sum_sem.at[which, 0, n],
            R.sum_sem.at[which, 1, n],
            "tensor",
            peer,
        )

    def sum_start(which, bank, value=None):
        if value is not None:
            R.sum_src[bank] = value.reshape(n_ten, 2, own_rows // 2, model)
        for n in range(4):
            sum_copy(which, bank, n).start()

    def sum_relay(which, bank):
        sum_copy(which, bank, 0).wait_recv()
        R.sum_via[bank, 0] = R.sum_slots[bank, 0] + R.sum_src[bank, over_ten, 0]
        sum_copy(which, bank, 4).start()
        sum_copy(which, bank, 1).wait_recv()
        R.sum_via[bank, 1] = R.sum_slots[bank, 1] + R.sum_src[bank, near_ten, 1]
        sum_copy(which, bank, 5).start()

    def sum_end(which, bank):
        for n in range(2, 6):
            sum_copy(which, bank, n).wait_recv()
        slots = R.sum_slots
        own = R.sum_src
        return jnp.concatenate(
            [
                own[bank, ten, 0] + slots[bank, 2] + slots[bank, 4],
                own[bank, ten, 1] + slots[bank, 3] + slots[bank, 5],
            ],
            axis=0,
        )

    def sum_sent(which, bank):
        for n in range(6):
            sum_copy(which, bank, n).wait_send()

    def share_copy(which, n, arriving=False):
        if arriving:
            owner = (near_ten, over_ten, near_ten, over_ten, far_ten, far_ten)[n]
        else:
            owner = (ten, ten, ten, ten, near_ten, over_ten)[n]
        spot = R.shared.at[min(which, 3), owner, (0, 1, 1, 0, 0, 1)[n]]
        return remote(
            spot,
            spot,
            R.share_sem.at[which, 0, n],
            R.share_sem.at[which, 1, n],
            "tensor",
            (near_ten, over_ten, near_ten, over_ten, over_ten, near_ten)[n],
        )

    def share_start(which, value=None):
        if value is not None:
            R.shared[which, ten] = value.reshape(2, own_rows // 2, model)
        for n in range(4):
            share_copy(which, n).start()

    def share_relay(which):
        share_copy(which, 0, True).wait_recv()
        share_copy(which, 4).start()
        share_copy(which, 1, True).wait_recv()
        share_copy(which, 5).start()

    def share_end(which):
        for n in range(2, 6):
            share_copy(which, n, True).wait_recv()

    def share_sent(which):
        for n in range(6):
            share_copy(which, n).wait_send()

    arrays = len(pieces)
    cut = (1, 1, 0, 0, 0)
    heights = [R.made(i).shape[1] for i in range(arrays)]

    def rows(i, piece):
        height = heights[i] // pieces[i]
        return pl.ds(piece * height, height)

    def near_copy(i, step, dest, piece):
        peer = lax.rem(ctx + step, n_ctx)
        return remote(
            R.made(i).at[peer * n_dp + dest, rows(i, piece)],
            R.near(i).at[step - 1, dest, rows(i, piece)],
            R.near_sem(i).at[0, step - 1, dest, piece],
            R.near_sem(i).at[1, step - 1, dest, piece],
            "context",
            peer,
        )

    def line_copy(i, way, dest, piece, peer):
        goal = jnp.where(dest == peer, n_dp, dest) if way == 1 else dest
        return remote(
            R.line(i).at[dest, rows(i, piece)],
            R.line(i).at[goal, rows(i, piece)],
            R.line_sem(i).at[0, way, dest, piece],
            R.line_sem(i).at[1, way, dest, piece],
            "dp",
            peer,
        )

    def loop(low, high, body):
        if high - low == 1:
            body(low)
        else:

            def lap(index, carry):
                body(index)
                return carry

            lax.fori_loop(low, high, lap, 0)

    def over_pieces(i, body):
        loop(0, pieces[i], body)

    def over_steps(body):
        loop(1, n_ctx, body)

    def takes_part(i, dest):
        if not cut[i]:
            return True
        if dest == 0:
            return dp < last
        if dest == last:
            return dp > 0
        return jnp.logical_not(is_end)

    def guarded(condition, body):
        if condition is True:
            body()
        else:
            pl.when(condition)(body)

    def put(i, owner, dest):
        made = R.made(i)
        cols = pl.ds(pl.multiple_of(owner * part, part), part) if wide else None
        if i < 2:
            right = R.mixed if i == 0 else R.gpair
            left = R.g_s if i == 0 else R.n2_s
            both = jnp.logical_or(
                dp == 1 if dest >= 1 else False, dp == last - 1 if dest < last else False
            )

            @pl.when(both)
            def _():
                if wide:
                    made[owner] = mm(right[...], left[:, cols])
                else:
                    made[owner] = mm_nt(R.left(i)[owner], right[...])

            @pl.when(jnp.logical_not(both))
            def _():
                if wide:
                    made[owner] = mm(right[:, :tokens], left[:tokens, cols])
                else:
                    made[owner] = mm_nt(R.left(i)[owner, :, :tokens], right[:, :tokens])

        elif i == 2:
            if wide:
                made[owner] = mm(R.gated[...], R.n2_s[:tokens, cols])
            else:
                made[owner] = mm_nt(R.left0[owner, :, :tokens], R.gated[...])
        elif i == 3:
            made[owner] = mm(R.left3[owner], R.gproj[...])

    def make(i, dest):
        def body():
            def step_body(step):
                put(i, lax.rem(ctx + step, n_ctx) * n_dp + dest, dest)
                over_pieces(i, lambda piece: near_copy(i, step, dest, piece).start())

            over_steps(step_body)
            put(i, ctx * n_dp + dest, dest)

        guarded(takes_part(i, dest), body)

    def own_sum(i, dest, piece):
        total = R.made(i)[ctx * n_dp + dest, rows(i, piece)]
        for step in range(1, n_ctx):
            near_copy(i, step, dest, piece).wait_recv()
            total = total + R.near(i)[step - 1, dest, rows(i, piece)]
        return total

    def first_send(i, way, dest):
        start = cut[i] if way == 0 else last - cut[i]
        if dest <= start if way == 0 else dest >= start:
            return

        @pl.when(dp == start)
        def _():
            def body(piece):
                R.line(i)[dest, rows(i, piece)] = own_sum(i, dest, piece)
                line_copy(i, way, dest, piece, dp + 1 if way == 0 else dp - 1).start()

            over_pieces(i, body)

    def middle_send(i, way, dest, hop):
        reach = dest - cut[i] if way == 0 else last - cut[i] - dest
        if reach < (2 if hop == 1 else 3):
            return
        if way == 0:
            active = dp == cut[i] + 1
            if hop > 1:
                active = jnp.logical_and(dp > cut[i] + 1, dp < dest)
        else:
            active = dp == last - cut[i] - 1
            if hop > 1:
                active = jnp.logical_and(dp < last - cut[i] - 1, dp > dest)
        peer = dp + 1 if way == 0 else dp - 1

        @pl.when(active)
        def _():
            def body(piece):
                own = own_sum(i, dest, piece)
                line_copy(i, way, dest, piece, dp).wait_recv()
                R.line(i)[dest, rows(i, piece)] = (
                    R.line(i)[dest, rows(i, piece)] + own
                )
                line_copy(i, way, dest, piece, peer).start()

            over_pieces(i, body)

    def makes(i, k):
        for dest in dict.fromkeys((last - k, k)):
            make(i, dest)

    def firsts(i, k):
        first_send(i, 0, last - k)
        first_send(i, 1, k)

    def middles(i, k, hop):
        middle_send(i, 0, last - k, hop)
        middle_send(i, 1, k, hop)

    laps = -(-n_dp // 2)

    def build(i, begin=0):
        for k in range(begin, laps):
            makes(i, k)
            firsts(i, k)
        for k in range(laps, last):
            firsts(i, k)

    def finish(i, out):
        def body(piece):
            span = rows(i, piece)
            here = ctx * n_dp + dp
            made = R.made(i)
            made[here, span] = own_sum(i, dp, piece)

            @pl.when(dp > cut[i])
            def _():
                line_copy(i, 0, dp, piece, dp).wait_recv()
                made[here, span] += R.line(i)[dp, span]

            @pl.when(dp < last - cut[i])
            def _():
                line_copy(i, 1, dp, piece, dp).wait_recv()
                made[here, span] += R.line(i)[n_dp, span]

            out(span, made[here, span])

        over_pieces(i, body)

    def drain(i):
        for dest in range(n_dp):

            def near_sent(dest=dest):
                def body(piece):
                    for step in range(1, n_ctx):
                        near_copy(i, step, dest, piece).wait_send()

                over_pieces(i, body)

            guarded(takes_part(i, dest), near_sent)
            if dest > cut[i]:

                @pl.when(jnp.logical_and(dp >= cut[i], dp < dest))
                def _(dest=dest):
                    over_pieces(
                        i, lambda piece: line_copy(i, 0, dest, piece, dp + 1).wait_send()
                    )

            if dest < last - cut[i]:

                @pl.when(jnp.logical_and(dp <= last - cut[i], dp > dest))
                def _(dest=dest):
                    over_pieces(
                        i, lambda piece: line_copy(i, 1, dest, piece, dp - 1).wait_send()
                    )

    def turned(value):
        return value.T.reshape(owners, part, value.shape[0]).astype(bf16)

    sum_start(0, 0, mm(gated.astype(bf16), R.wo_s[...]))
    R.gated[...] = gated.T.astype(bf16)
    sum_relay(0, 0)
    R.left3[...] = turned(norm_one()[1].astype(f32))
    hid = R.x_s[mine, :].astype(f32) + sum_end(0, 0)
    R.hid[...] = hid
    gain2 = R.gain2[...]
    share_start(0, (hid * rms_scale(hid) * gain2).astype(bf16).astype(f32))

    @pl.when(is_end)
    def _():
        ext_copy(1, end_peer).start()

    load("wg").wait()
    load("wu").wait()
    load("wd").wait()
    sum_sent(0, 0)
    share_relay(0)
    R.gm[...] = mm_nt(R.wd_s[...], R.g_s[:tokens, :])

    @pl.when(absorbs)
    def _():
        ext_copy(0, absorb_peer).wait_recv()
        R.g_s[tokens:, :] = R.shared[2].reshape(tokens, model).astype(bf16)
        ext_copy(1, absorb_peer).wait_recv()
        share_start(4)

    share_end(0)

    def feed_forward(half):
        span = slice(half * tokens, (half + 1) * tokens)
        n2 = R.n2_s[span, :]
        ffn_gate = mm_nt(R.wgu[:hidden, :], n2)
        ffn_up = mm_nt(R.wgu[hidden:, :], n2)
        R.mixed[:, span] = (ffn_gate * jax.nn.sigmoid(ffn_gate) * ffn_up).astype(bf16)
        R.ffn_gate[...] = ffn_gate
        R.ffn_up[...] = ffn_up

    def feed_back(half):
        span = slice(half * tokens, (half + 1) * tokens)
        grad_mixed, ffn_gate, ffn_up = R.gm[...], R.ffn_gate[...], R.ffn_up[...]
        sig = jax.nn.sigmoid(ffn_gate)
        R.gpair[:hidden, span] = (
            grad_mixed * ffn_up * (sig * (1.0 + ffn_gate * (1.0 - sig)))
        ).astype(bf16)
        R.gpair[hidden:, span] = (grad_mixed * (ffn_gate * sig)).astype(bf16)

    R.n2_s[:tokens, :] = R.shared[0].reshape(tokens, model).astype(bf16)
    feed_forward(0)
    feed_back(0)

    @pl.when(absorbs)
    def _():
        share_relay(4)
        R.gm[...] = mm_nt(R.wd_s[...], R.g_s[tokens:, :])

    ffn_part = mm_tn(R.gpair[:, :tokens], R.wgu[...])
    R.sum_src[0] = ffn_part.reshape(R.sum_src.shape[1:])

    @pl.when(absorbs)
    def _():
        share_end(4)

    sum_start(1, 0)

    @pl.when(absorbs)
    def _():
        R.n2_s[tokens:, :] = R.shared[3].reshape(tokens, model).astype(bf16)
        feed_forward(1)

    if not wide:
        for at in range(0, 2 * tokens, 128):
            span = slice(at, at + 128)
            R.left0[:, :, span] = turned(R.g_s[span, :].astype(f32))
            R.left1[:, :, span] = turned(R.n2_s[span, :].astype(f32))
    makes(0, 0)
    sum_relay(1, 0)
    firsts(0, 0)

    @pl.when(absorbs)
    def _():
        feed_back(1)

    grad_normed_two = sum_end(1, 0)
    hid = R.hid[...]
    grad_two_rows, gain_two_part = norm_back(hid, rms_scale(hid), gain2, grad_normed_two)
    grad_hidden = R.g_s[mine, :].astype(f32) + grad_two_rows
    R.gh[...] = grad_hidden
    share_start(1, grad_hidden.astype(bf16).astype(f32))
    sum_sent(1, 0)
    build(0, 1)
    share_relay(1)

    @pl.when(is_end)
    def _():
        ext_copy(0, end_peer).wait_send()

    sum_start(2, 1, mm_tn(R.mixed[:, :tokens], R.wd_s[...]))
    build(1)
    middles(0, 0, 1)
    share_end(1)

    R.n2_s[:tokens, :] = R.shared[1].reshape(tokens, model).astype(bf16)
    grad_gated = mm_nt(R.n2_s[:tokens, :], R.wo_s[...])
    o = R.o_s[...]
    gate_in = R.proj[:, 2 * key_dim + value_dim :]
    scale_h = lax.rsqrt(jnp.mean(o * o, axis=-1, keepdims=True) + EPS_HEAD)
    sig = jax.nn.sigmoid(gate_in)
    soft = gate_in * sig
    hgain = R.hgain[...]
    normal = o * scale_h
    head_part = jnp.sum(grad_gated * normal * soft, axis=0, keepdims=True)
    R.gproj[:, 2 * key_dim + value_dim :] = (
        grad_gated * normal * hgain * (sig * (1.0 + gate_in * (1.0 - sig)))
    ).astype(bf16)
    back = grad_gated * hgain * soft
    go = scale_h * (
        back - normal * scale_h * jnp.mean(back * o, axis=-1, keepdims=True)
    )
    R.go[...] = go
    R.pair_back[:, :value_dim] = hdot(R.decayed[...], go, ((0,), (0,)))
    R.pair_back[:, value_dim:] = R.pair[:, value_dim:]
    for step in range(1, n_ctx):
        ctx_copy(1, R.pair_back, R.back_slots, step).start()
    sum_relay(2, 1)
    if not wide:
        R.left0[:, :, :tokens] = turned(R.shared[1].reshape(tokens, model))
    build(2)
    for step in range(1, n_ctx):
        ctx_copy(1, R.pair_back, R.back_slots, step).wait_recv()
    fold(R.later, R.back_slots, True)
    gla_backward(
        R.proj, R.cumuls, R.states, R.entry, R.later, R.go, R.gproj, R.dr
    )
    grad_logits = R.dr[...] * jax.nn.sigmoid(-R.logits[...]) / GATE_NORM
    grad_low = hdot(grad_logits, R.wlu[...].astype(f32), ((1,), (1,)))

    @pl.when(absorbs)
    def _():
        share_sent(4)

    sum_start(
        3,
        0,
        mm_nt(R.gproj[...], R.wcat[...])
        + hdot(grad_low, R.wld[...].astype(f32), ((1,), (0,))),
    )
    scaled, n1f = norm_one()
    low_down = hdot(grad_low, n1f.astype(f32), ((0,), (0,)))
    low_up = hdot(R.low[...], grad_logits, ((0,), (0,)))
    bias_part = jnp.sum(grad_logits, axis=0, keepdims=True)
    gain_one_part = jnp.sum(
        R.sum_src[0].reshape(tokens, model) * scaled, axis=0, keepdims=True
    )
    R.made4[...] = jnp.zeros_like(R.made4)
    part_head = value_dim // owners
    part_key = key_dim // owners
    tail = R.tail_slots.shape[1]
    for owner in range(owners):
        span = slice(owner * part, (owner + 1) * part)
        R.made4[owner, :rank, :part] = low_down[:, span]
        R.made4[owner, rank : rank + 1, :part] = gain_one_part[:, span]
        R.made4[owner, rank + 1 : rank + 2, :part] = gain_two_part[:, span]
        R.made4[owner, rank + 2 : rank + 3, :part_head] = head_part[
            :, owner * part_head : (owner + 1) * part_head
        ]
        span = slice(owner * part_key, (owner + 1) * part_key)
        R.made4[owner, tail : tail + rank, :part_key] = low_up[:, span]
        R.made4[owner, tail + rank : tail + rank + 1, :part_key] = bias_part[:, span]
    build(4)
    build(3)
    sum_relay(3, 0)
    for k in range(last):
        middles(2, k, 1)
    for k in range(last):
        middles(4, k, 1)
    middles(1, 0, 1)
    result = R.hid[...] + sum_end(2, 1)
    share_start(2, result.astype(bf16).astype(f32))
    middles(3, 0, 1)
    grad_normed_one = sum_end(3, 0)
    own_in = R.x_s[mine, :].astype(f32)
    grad_one_rows, _ = norm_back(own_in, rms_scale(own_in), R.gain1[...], grad_normed_one)
    share_relay(2)
    share_start(3, R.gh[...] + grad_one_rows)
    for i in range(2):
        for k in range(1, last):
            middles(i, k, 1)
    for k in range(1, last):
        middles(3, k, 1)
    share_relay(3)
    for i in (0, 1, 2, 4, 3):
        for k in range(last):
            middles(i, k, 2)

    def into(name):
        def out(span, value):
            getattr(R, name)[span, :] = value

        return out

    def put_proj(span, value):
        R.gq[span, :] = value[:, :key_dim]
        R.gk[span, :] = value[:, key_dim : 2 * key_dim]
        R.gv[span, :] = value[:, 2 * key_dim : 2 * key_dim + value_dim]
        R.ggo[span, :] = value[:, 2 * key_dim + value_dim :]

    def leave(name):
        return pltpu.make_async_copy(
            getattr(R, name), getattr(R, "out_" + name), R.leave_sem.at[LEAVES.index(name)]
        )

    finish(0, into("gdown"))
    leave("gdown").start()
    finish(1, into("gpairs"))
    leave("gpairs").start()
    share_end(2)
    R.result[...] = R.shared[2].reshape(tokens, model).astype(bf16)
    leave("result").start()
    share_end(3)
    R.gin[...] = R.shared[3].reshape(tokens, model)
    leave("gin").start()
    finish(2, into("gout"))
    leave("gout").start()
    finish(4, into("pack"))
    R.tail_slots[ten] = R.pack[:tail, :]

    def tail_copy(sender, peer, step):
        spot = R.tail_slots.at[sender]
        return remote(
            spot, spot, R.tail_sem.at[0, step - 1], R.tail_sem.at[1, step - 1], "tensor", peer
        )

    for step in range(1, n_ten):
        tail_copy(ten, lax.rem(ten + step, n_ten), step).start()
    finish(3, put_proj)
    for name in ("gq", "gk", "gv", "ggo"):
        leave(name).start()
    for step in range(1, n_ten):
        sender = lax.rem(ten + n_ten - step, n_ten)
        tail_copy(sender, sender, step).wait_recv()
    total = R.tail_slots[0]
    for index in range(1, n_ten):
        total = total + R.tail_slots[index]
    R.pack[:tail, :] = total
    leave("pack").start()

    for step in range(1, n_ctx):
        ctx_copy(0, R.pair, R.pair_slots, step).wait_send()
        ctx_copy(1, R.pair_back, R.back_slots, step).wait_send()
    sum_sent(2, 1)
    sum_sent(3, 0)
    for which in range(4):
        share_sent(which)

    @pl.when(is_end)
    def _():
        ext_copy(1, end_peer).wait_send()

    for i in range(arrays):
        drain(i)
    for step in range(1, n_ten):
        tail_copy(ten, lax.rem(ten + step, n_ten), step).wait_send()
    for name in LEAVES:
        leave(name).wait()


def hand_out_kernel(moves, n_in, n_big, *refs):
    ins, pack_ref = refs[: n_in - 1], refs[n_in - 1]
    big = refs[n_in : n_in + n_big]
    small = refs[n_in + n_big : n_in + n_big + 6]
    held = refs[n_in + n_big + 6 : -1]
    sems = refs[-1]

    def arrive(at):
        return pltpu.make_async_copy(ins[at], held[at], sems.at[0, at])

    def depart(at):
        source, first, rows = moves[at]
        src = held[source] if rows is None else held[source].at[first : first + rows]
        return pltpu.make_async_copy(src, big[at], sems.at[1, at])

    for at in range(len(ins)):
        arrive(at).start()
    for at in range(len(ins)):
        arrive(at).wait()
        for move in range(n_big):
            if moves[move][0] == at:
                depart(move).start()
    low_down, gain1, gain2, hgain, low_up, bias = small
    rank, part = low_down.shape
    tail = -(-(rank + 3) // 8) * 8
    low_down[...] = pack_ref[:rank, :part]
    gain1[...] = pack_ref[rank : rank + 1, :part]
    gain2[...] = pack_ref[rank + 1 : rank + 2, :part]
    hgain[...] = pack_ref[rank + 2 : rank + 3, : hgain.shape[1]]
    low_up[...] = pack_ref[tail : tail + rank, : low_up.shape[1]]
    bias[...] = pack_ref[tail + rank : tail + rank + 1, : bias.shape[1]]
    for at in range(n_big):
        depart(at).wait()


def shards(
    inputs,
    norm_gain1,
    w_query,
    w_key,
    w_value,
    w_gate_out,
    w_low_down,
    w_low_up,
    forget_bias,
    head_gain,
    w_output,
    norm_gain2,
    w_ffn_gate,
    w_ffn_up,
    w_ffn_down,
    cotangent,
):
    bf16, f32 = jnp.bfloat16, jnp.float32
    n_ctx, n_dp, n_ten = (lax.axis_size(axis) for axis in ("context", "dp", "tensor"))
    owners = n_ctx * n_dp
    model = inputs.shape[-1]
    x = inputs.reshape(-1, model)
    tokens = x.shape[0]
    key_dim, value_dim, hidden = w_query.shape[1], w_value.shape[1], w_ffn_gate.shape[1]
    assert inputs.shape[0] == 1 and head_gain.shape[0] == value_dim
    assert n_ten == 4 and n_dp >= 4
    rank = w_low_down.shape[1]
    part = model // owners
    wide = part % 128 == 0
    own_rows = tokens // n_ten
    width = 2 * key_dim + 2 * value_dim
    tail = -(-(rank + 3) // 8) * 8
    pack_rows = tail + -(-(rank + 1) // 8) * 8

    ins = dict(
        x=x,
        gain1=norm_gain1[None],
        wq=w_query,
        wk=w_key,
        wv=w_value,
        wgo=w_gate_out,
        wld=w_low_down.T,
        wlu=w_low_up,
        bias=forget_bias[None],
        hgain=head_gain[None],
        wo=w_output,
        gain2=norm_gain2[None],
        wg=w_ffn_gate.T,
        wu=w_ffn_up.T,
        wd=w_ffn_down,
        g=cotangent.reshape(-1, model),
    )

    def owned(extent):
        return (extent, part) if wide else (part, extent)

    shapes = [owned(hidden), owned(2 * hidden), owned(value_dim), (part, width), (pack_rows, 128)]
    outs = dict(
        result=((tokens, model), bf16),
        gin=((tokens, model), f32),
        gq=((part, key_dim), f32),
        gk=((part, key_dim), f32),
        gv=((part, value_dim), f32),
        ggo=((part, value_dim), f32),
        gout=(shapes[2], f32),
        gpairs=(shapes[1], f32),
        gdown=(shapes[0], f32),
        pack=((pack_rows, 128), f32),
    )
    pieces = []
    for shape in shapes:
        count = 4
        while shape[0] % (count * 8):
            count //= 2
        pieces.append(count if shape[0] * shape[1] > 16384 else 1)

    dma = pltpu.SemaphoreType.DMA
    scratch = dict(
        x_s=pltpu.VMEM((tokens, model), bf16),
        g_s=pltpu.VMEM((2 * tokens, model), bf16),
        ext_sem=dma((2, 2)),
        wcat=pltpu.VMEM((model, width), bf16),
        wo_s=pltpu.VMEM((value_dim, model), bf16),
        wgu=pltpu.VMEM((2 * hidden, model), bf16),
        wd_s=pltpu.VMEM((hidden, model), bf16),
        load_sem=dma((len(LOADS),)),
        leave_sem=dma((len(LEAVES),)),
        n2_s=pltpu.VMEM((2 * tokens, model), bf16),
        proj=pltpu.VMEM((tokens, width), f32),
        low=pltpu.VMEM((tokens, rank), f32),
        logits=pltpu.VMEM((tokens, key_dim), f32),
        rates=pltpu.VMEM((tokens, key_dim), f32),
        cumuls=pltpu.VMEM((tokens, key_dim), f32),
        o_s=pltpu.VMEM((tokens, value_dim), f32),
        decayed=pltpu.VMEM((tokens, key_dim), f32),
        states=pltpu.VMEM((tokens // BLOCK, key_dim, value_dim), f32),
        pair=pltpu.VMEM((key_dim, value_dim + key_dim), f32),
        pair_back=pltpu.VMEM((key_dim, value_dim + key_dim), f32),
        pair_slots=pltpu.VMEM((n_ctx - 1, key_dim, value_dim + key_dim), f32),
        back_slots=pltpu.VMEM((n_ctx - 1, key_dim, value_dim + key_dim), f32),
        ctx_sem=dma((2, 2, n_ctx - 1)),
        entry=pltpu.VMEM((key_dim, value_dim), f32),
        later=pltpu.VMEM((key_dim, value_dim), f32),
        gm=pltpu.VMEM((hidden, tokens), f32),
        ffn_gate=pltpu.VMEM((hidden, tokens), f32),
        ffn_up=pltpu.VMEM((hidden, tokens), f32),
        gated=pltpu.VMEM((value_dim, tokens), bf16),
        sum_src=pltpu.VMEM((2, n_ten, 2, own_rows // 2, model), f32),
        sum_slots=pltpu.VMEM((2, 6, own_rows // 2, model), f32),
        sum_via=pltpu.VMEM((2, 2, own_rows // 2, model), f32),
        sum_sem=dma((4, 2, 6)),
        shared=pltpu.VMEM((4, n_ten, 2, own_rows // 2, model), f32),
        share_sem=dma((5, 2, 6)),
        hid=pltpu.VMEM((own_rows, model), f32),
        gh=pltpu.VMEM((own_rows, model), f32),
        mixed=pltpu.VMEM((hidden, 2 * tokens), bf16),
        gpair=pltpu.VMEM((2 * hidden, 2 * tokens), bf16),
        go=pltpu.VMEM((tokens, value_dim), f32),
        dr=pltpu.VMEM((tokens, key_dim), f32),
        gproj=pltpu.VMEM((tokens, width), bf16),
        tail_slots=pltpu.VMEM((n_ten, tail, 128), f32),
        tail_sem=dma((2, n_ten - 1)),
        left3=pltpu.VMEM((owners, part, tokens), bf16),
    )
    if not wide:
        scratch["left0"] = pltpu.VMEM((owners, part, 2 * tokens), bf16)
        scratch["left1"] = pltpu.VMEM((owners, part, 2 * tokens), bf16)
    for i, shape in enumerate(shapes):
        scratch["made%d" % i] = pltpu.VMEM((owners,) + shape, f32)
        scratch["near%d" % i] = pltpu.VMEM((n_ctx - 1, n_dp) + shape, f32)
        scratch["line%d" % i] = pltpu.VMEM((n_dp + 1,) + shape, f32)
        scratch["near_sem%d" % i] = dma((2, n_ctx - 1, n_dp, pieces[i]))
        scratch["line_sem%d" % i] = dma((2, 2, n_dp, pieces[i]))

    for name in LEAVES:
        scratch[name] = pltpu.VMEM(*outs[name])
    names = tuple(ins) + tuple("out_" + name for name in outs) + tuple(scratch)
    made = pl.pallas_call(
        functools.partial(block_kernel, (n_ctx, n_dp, n_ten), names, tuple(pieces), wide),
        out_shape=tuple(jax.ShapeDtypeStruct(shape, kind) for shape, kind in outs.values()),
        in_specs=[
            pl.BlockSpec(memory_space=pl.ANY if name in LOADS else VMEM) for name in ins
        ],
        out_specs=tuple([pl.BlockSpec(memory_space=pl.ANY)] * len(outs)),
        scratch_shapes=list(scratch.values()),
        compiler_params=pltpu.CompilerParams(
            collective_id=0, has_side_effects=True, vmem_limit_bytes=VMEM_LIMIT
        ),
        name="gla_block",
    )(*ins.values())
    part_head = value_dim // owners
    part_key = key_dim // owners
    moves, big_shapes = [], []
    for at, name in enumerate(list(outs)[:-1]):
        shape, kind = outs[name]
        if name == "gpairs" and wide:
            for half in range(2):
                moves.append((at, half * hidden, hidden))
                big_shapes.append(((hidden, part), kind))
        else:
            moves.append((at, 0, None))
            big_shapes.append((shape, kind))
    small_shapes = [
        (rank, part),
        (1, part),
        (1, part),
        (1, part_head),
        (rank, part_key),
        (1, part_key),
    ]
    done = pl.pallas_call(
        functools.partial(hand_out_kernel, tuple(moves), len(made), len(moves)),
        out_shape=tuple(
            [jax.ShapeDtypeStruct(shape, kind) for shape, kind in big_shapes]
            + [jax.ShapeDtypeStruct(shape, f32) for shape in small_shapes]
        ),
        in_specs=[pl.BlockSpec(memory_space=pl.ANY)] * (len(made) - 1)
        + [pl.BlockSpec(memory_space=VMEM)],
        out_specs=tuple(
            [pl.BlockSpec(memory_space=pl.ANY)] * len(moves)
            + [pl.BlockSpec(memory_space=VMEM)] * len(small_shapes)
        ),
        scratch_shapes=[pltpu.VMEM(shape, kind) for shape, kind in list(outs.values())[:-1]]
        + [dma((2, len(moves)))],
        name="hand_out",
    )(*made)
    low_down, gain1, gain2, hgain, low_up, bias = done[len(moves) :]
    result, gin, gq, gk, gv, ggo, gout = done[:7]
    if wide:
        ggate, gup, gdown = done[7].T, done[8].T, done[9]
    else:
        ggate, gup = done[7][:, :hidden], done[7][:, hidden:]
        gdown, gout = done[8].T, gout.T
    return (
        result.reshape(inputs.shape),
        gin.reshape(inputs.shape),
        gain1.reshape(-1),
        gq,
        gk,
        gv,
        ggo,
        low_down.T,
        low_up,
        bias.reshape(-1),
        hgain.reshape(-1),
        gout,
        gain2.reshape(-1),
        ggate,
        gup,
        gdown,
    )


def solution(mesh):
    return jax.shard_map(
        shards,
        mesh=mesh,
        in_specs=(
            P("dp", "context", None),
            P(),
            P(None, "tensor"),
            P(None, "tensor"),
            P(None, "tensor"),
            P(None, "tensor"),
            P(),
            P(None, "tensor"),
            P("tensor"),
            P(),
            P("tensor", None),
            P(),
            P(None, "tensor"),
            P(None, "tensor"),
            P("tensor", None),
            P("dp", "context", None),
        ),
        out_specs=(
            P("dp", "context", None),
            P("dp", "context", None),
            P(("context", "dp")),
            P(("context", "dp"), "tensor"),
            P(("context", "dp"), "tensor"),
            P(("context", "dp"), "tensor"),
            P(("context", "dp"), "tensor"),
            P(("context", "dp"), None),
            P(None, ("tensor", "context", "dp")),
            P(("tensor", "context", "dp")),
            P(("context", "dp")),
            P("tensor", ("context", "dp")),
            P(("context", "dp")),
            P(("context", "dp"), "tensor"),
            P(("context", "dp"), "tensor"),
            P("tensor", ("context", "dp")),
        ),
        check_vma=False,
    )
```

```python
import functools

import jax
import jax.numpy as jnp
from jax import lax
from jax.experimental import pallas as pl
from jax.experimental.pallas import tpu as pltpu
from jax.sharding import PartitionSpec as P

BLOCK = 64


EPS_MODEL = 1e-06
EPS_HEAD = 1e-05
GATE_NORM = 16.0
HIGHEST = lax.Precision.HIGHEST


VMEM_LIMIT = 63 * 1024 * 1024
VMEM = pltpu.MemorySpace.VMEM
MESH_ID = pl.DeviceIdType.MESH


def hdot(left, right, dims):
    return lax.dot_general(
        left, right, (dims, ((), ())), precision=HIGHEST, preferred_element_type=jnp.float32
    )


def hdot3(left, right, dims):
    f32, bf16 = jnp.float32, jnp.bfloat16

    def halves(value):
        high = value.astype(bf16)
        return high, (value - high.astype(f32)).astype(bf16)

    def dot(one, two):
        return lax.dot_general(one, two, (dims, ((), ())), preferred_element_type=f32)

    (left_high, left_low), (right_high, right_low) = halves(left), halves(right)
    return dot(left_high, right_high) + (dot(left_high, right_low) + dot(left_low, right_high))


def mm(left, right):
    return jnp.dot(left, right, preferred_element_type=jnp.float32)


def mm_nt(left, right):
    return lax.dot_general(
        left, right, (((1,), (1,)), ((), ())), preferred_element_type=jnp.float32
    )


def column_of(row, height):
    return jnp.broadcast_to(row, (height, row.shape[1])).T


def triangle(length):
    rows = lax.broadcasted_iota(jnp.int32, (length, length), 0)
    cols = lax.broadcasted_iota(jnp.int32, (length, length), 1)
    return rows >= cols


def rms_scale(rows_in):
    return lax.rsqrt(jnp.mean(rows_in * rows_in, axis=-1, keepdims=True) + EPS_MODEL)


def norm_back(rows_in, scale_rows, gain_in, grad_normed):
    weighted = gain_in * grad_normed
    grad_gain = jnp.sum(grad_normed * rows_in * scale_rows, axis=0, keepdims=True)
    grad_rows = scale_rows * (
        weighted
        - rows_in * scale_rows * scale_rows * jnp.mean(weighted * rows_in, axis=-1, keepdims=True)
    )
    return (grad_rows, grad_gain)


def gla_states(proj, rates, cumuls_ref, states_ref, pair_ref):
    tokens, key_dim = rates.shape
    value_dim = states_ref.shape[2]
    ones_low = triangle(BLOCK).astype(jnp.float32)
    state = jnp.zeros((key_dim, value_dim), jnp.float32)
    before = jnp.zeros((1, key_dim), jnp.float32)
    for block in range(tokens // BLOCK):
        span = pl.ds(block * BLOCK, BLOCK)
        keys_in = proj[span, key_dim : 2 * key_dim]
        values_in = proj[span, 2 * key_dim : 2 * key_dim + value_dim]
        cumul = hdot(ones_low, rates[span, :], ((1,), (0,)))
        cumuls_ref[span, :] = cumul
        end_log = cumul[BLOCK - 1 :, :]
        states_ref[block] = state
        added = hdot3(keys_in * jnp.exp(end_log - cumul), values_in, ((0,), (0,)))
        state = column_of(jnp.exp(end_log), key_dim)[:, :1] * state + added
        before = before + end_log
    pair_ref[:, :value_dim] = state
    pair_ref[:, value_dim:] = column_of(jnp.exp(before), key_dim)


def gla_outputs(proj, cumuls_ref, states_ref, out_ref, decayed_ref):
    tokens, key_dim = cumuls_ref.shape
    value_dim = states_ref.shape[2]
    causal = triangle(BLOCK)
    before = jnp.zeros((1, key_dim), jnp.float32)
    for block in range(tokens // BLOCK):
        span = pl.ds(block * BLOCK, BLOCK)
        queries = proj[span, :key_dim]
        keys_in = proj[span, key_dim : 2 * key_dim]
        values_in = proj[span, 2 * key_dim : 2 * key_dim + value_dim]
        cumul = cumuls_ref[span, :]
        end_log = cumul[BLOCK - 1 :, :]
        anchor = 0.5 * end_log
        scores = hdot3(
            queries * jnp.exp(cumul - anchor), keys_in * jnp.exp(anchor - cumul), ((1,), (1,))
        )
        scores = jnp.where(causal, scores, 0.0)
        out_ref[span, :] = hdot3(scores, values_in, ((1,), (0,))) + hdot3(
            queries * jnp.exp(cumul), states_ref[block], ((1,), (0,))
        )
        decayed_ref[span, :] = queries * jnp.exp(cumul + before)
        before = before + end_log


def gla_backward(proj, cumuls_ref, states_ref, entry_ref, later_ref, g_ref, dqkv_ref, dr_ref):
    tokens, key_dim = cumuls_ref.shape
    value_dim = g_ref.shape[1]
    causal = triangle(BLOCK)
    ones_low = causal.astype(jnp.float32)
    blocks = tokens // BLOCK
    cumuls, befores = [], []
    before = jnp.zeros((1, key_dim), jnp.float32)
    for block in range(blocks):
        cumul = cumuls_ref[pl.ds(block * BLOCK, BLOCK), :]
        cumuls.append(cumul)
        befores.append(before)
        before = before + cumul[BLOCK - 1 :, :]
    grad_state = later_ref[...]
    entry = entry_ref[...]
    for block in reversed(range(blocks)):
        span = pl.ds(block * BLOCK, BLOCK)
        queries = proj[span, :key_dim]
        keys_in = proj[span, key_dim : 2 * key_dim]
        values_in = proj[span, 2 * key_dim : 2 * key_dim + value_dim]
        grad_out = g_ref[span, :]
        cumul = cumuls[block]
        end_log = cumul[BLOCK - 1 :, :]
        anchor = 0.5 * end_log
        state = states_ref[block] + column_of(jnp.exp(befores[block]), key_dim)[:, :1] * entry
        up, down = jnp.exp(cumul - anchor), jnp.exp(anchor - cumul)
        grow, rest = jnp.exp(cumul), jnp.exp(end_log - cumul)
        q_up, k_down = queries * up, keys_in * down
        scores = jnp.where(causal, hdot(q_up, k_down, ((1,), (1,))), 0.0)
        grad_scores = jnp.where(causal, hdot(grad_out, values_in, ((1,), (1,))), 0.0)
        grad_q = hdot(grad_scores, k_down, ((1,), (0,))) * up + grow * hdot(
            grad_out, state, ((1,), (1,))
        )
        carried_k = hdot(values_in, grad_state, ((1,), (1,))) * rest
        grad_k = hdot(grad_scores, q_up, ((0,), (0,))) * down + carried_k
        dqkv_ref[span, 2 * key_dim : 2 * key_dim + value_dim] = (
            hdot(scores, grad_out, ((0,), (0,)))
            + hdot(keys_in * rest, grad_state, ((1,), (0,)))
        ).astype(dqkv_ref.dtype)
        dqkv_ref[span, :key_dim] = (grad_q * key_dim ** (-0.5)).astype(dqkv_ref.dtype)
        dqkv_ref[span, key_dim : 2 * key_dim] = grad_k.astype(dqkv_ref.dtype)
        grad_cumul = queries * grad_q - keys_in * grad_k
        end_column = column_of(jnp.exp(end_log), key_dim)
        state_term = jnp.sum(grad_state * state, axis=1, keepdims=True) * end_column
        grad_end = state_term.T[:1, :] + jnp.sum(carried_k * keys_in, axis=0, keepdims=True)
        dr_ref[span, :] = hdot(ones_low, grad_cumul, ((0,), (0,))) + grad_end
        grad_state = end_column[:, :1] * grad_state + hdot(
            queries * grow, grad_out, ((0,), (0,))
        )


LEAVES = ("result", "gin", "gq", "gk", "gv", "ggo", "gout", "gpairs", "gdown", "pack")
LOADS = ("x", "wq", "wk", "wv", "wgo", "wo", "g", "wd", "wg", "wu")


class Refs:
    def __init__(self, pairs):
        self.__dict__.update(pairs)

    def made(self, i):
        return getattr(self, "made%d" % i)

    def near(self, i):
        return getattr(self, "near%d" % i)

    def line(self, i):
        return getattr(self, "line%d" % i)

    def near_sem(self, i):
        return getattr(self, "near_sem%d" % i)

    def line_sem(self, i):
        return getattr(self, "line_sem%d" % i)

    def left(self, i):
        return getattr(self, "left%d" % i)


def mm_tn(left, right):
    return lax.dot_general(
        left, right, (((0,), (0,)), ((), ())), preferred_element_type=jnp.float32
    )


def block_kernel(sizes, names, pieces, wide, *refs):
    f32, bf16 = jnp.float32, jnp.bfloat16
    n_ctx, n_dp, n_ten = sizes
    R = Refs(zip(names, refs))
    ctx = lax.axis_index("context")
    dp = lax.axis_index("dp")
    ten = lax.axis_index("tensor")
    tokens, model = R.x_s.shape
    key_dim = R.wq.shape[1]
    value_dim = R.wv.shape[1]
    hidden = R.wg.shape[0]
    rank = R.wld.shape[0]
    own_rows = tokens // n_ten
    owners = n_ctx * n_dp
    part = model // owners
    last = n_dp - 1
    mine = pl.ds(pl.multiple_of(ten * own_rows, own_rows), own_rows)
    near_ten = ten + 1 - 2 * lax.rem(ten, 2)
    over_ten = lax.rem(ten + 2, 4)
    far_ten = lax.rem(near_ten + 2, 4)
    is_end = jnp.logical_or(dp == 0, dp == last)
    absorbs = jnp.logical_or(dp == 1, dp == last - 1)
    end_peer = jnp.where(dp == 0, 1, last - 1)
    absorb_peer = jnp.where(dp == 1, 0, last)

    def remote(src, dst, send, recv, axis, peer):
        return pltpu.make_async_remote_copy(
            src_ref=src,
            dst_ref=dst,
            send_sem=send,
            recv_sem=recv,
            device_id={axis: peer},
            device_id_type=MESH_ID,
        )

    spots = dict(
        x=R.x_s,
        wq=R.wcat.at[:, :key_dim],
        wk=R.wcat.at[:, key_dim : 2 * key_dim],
        wv=R.wcat.at[:, 2 * key_dim : 2 * key_dim + value_dim],
        wgo=R.wcat.at[:, 2 * key_dim + value_dim :],
        wo=R.wo_s,
        g=R.g_s.at[:tokens],
        wd=R.wd_s,
        wg=R.wgu.at[:hidden],
        wu=R.wgu.at[hidden:],
    )

    def load(name):
        return pltpu.make_async_copy(getattr(R, name), spots[name], R.load_sem.at[LOADS.index(name)])

    for name in LOADS:
        load(name).start()

    barrier = pltpu.get_barrier_semaphore()

    def greet(axis, peer):
        pl.semaphore_signal(barrier, inc=1, device_id={axis: peer}, device_id_type=MESH_ID)

    for step in range(1, n_ctx):
        greet("context", lax.rem(ctx + step, n_ctx))
    for step in range(1, n_ten):
        greet("tensor", lax.rem(ten + step, n_ten))

    @pl.when(dp > 0)
    def _():
        greet("dp", dp - 1)

    @pl.when(dp < last)
    def _():
        greet("dp", dp + 1)

    load("x").wait()

    def norm_one():
        rows_in = R.x_s[...].astype(f32)
        scaled = rows_in * rms_scale(rows_in)
        return scaled, (scaled * R.gain1[...]).astype(bf16)

    n1f = norm_one()[1]
    for name in ("wq", "wk", "wv", "wgo"):
        load(name).wait()
    packed = mm(n1f, R.wcat[...])
    R.proj[:, :key_dim] = packed[:, :key_dim] * key_dim ** (-0.5)
    R.proj[:, key_dim:] = packed[:, key_dim:]
    expect = n_ctx + n_ten - 2

    @pl.when(jnp.logical_not(is_end))
    def _():
        pl.semaphore_wait(barrier, expect + 2)

    @pl.when(is_end)
    def _():
        pl.semaphore_wait(barrier, expect + 1)

    load("g").wait()
    R.sum_src[1] = R.g_s[:tokens, :].astype(f32).reshape(R.sum_src.shape[1:])

    def ext_copy(which, peer):
        if which == 0:
            src, dst = R.sum_src.at[1], R.shared.at[2]
        else:
            src, dst = R.shared.at[0, ten], R.shared.at[3, ten]
        return remote(src, dst, R.ext_sem.at[which, 0], R.ext_sem.at[which, 1], "dp", peer)

    @pl.when(is_end)
    def _():
        ext_copy(0, end_peer).start()

    low = mm_nt(n1f, R.wld[...])
    R.low[...] = low
    logits = hdot(low, R.wlu[...].astype(f32), ((1,), (0,))) + R.bias[...]
    R.logits[...] = logits
    R.rates[...] = (
        jnp.minimum(logits, 0.0) - jnp.log1p(jnp.exp(-jnp.abs(logits)))
    ) / GATE_NORM
    gla_states(R.proj, R.rates, R.cumuls, R.states, R.pair)

    def ctx_copy(which, src, slots, step):
        return remote(
            src,
            slots.at[step - 1],
            R.ctx_sem.at[which, 0, step - 1],
            R.ctx_sem.at[which, 1, step - 1],
            "context",
            lax.rem(ctx + step, n_ctx),
        )

    def fold(out_ref, slots, reverse):
        out_ref[...] = jnp.zeros_like(out_ref)
        for m in reversed(range(1, n_ctx)):
            index = n_ctx - m - 1 if reverse else m - 1

            @pl.when(ctx + m < n_ctx if reverse else ctx >= m)
            def _(index=index):
                out_ref[...] = (
                    slots[index, :, value_dim : value_dim + 1] * out_ref[...]
                    + slots[index, :, :value_dim]
                )

    for step in range(1, n_ctx):
        ctx_copy(0, R.pair, R.pair_slots, step).start()

    gla_outputs(R.proj, R.cumuls, R.states, R.o_s, R.decayed)
    for step in range(1, n_ctx):
        ctx_copy(0, R.pair, R.pair_slots, step).wait_recv()
    fold(R.entry, R.pair_slots, False)
    o = R.o_s[...] + hdot(R.decayed[...], R.entry[...], ((1,), (0,)))
    R.o_s[...] = o
    gate_in = R.proj[:, 2 * key_dim + value_dim :]
    scale_h = lax.rsqrt(jnp.mean(o * o, axis=-1, keepdims=True) + EPS_HEAD)
    gated = o * scale_h * R.hgain[...] * (gate_in * jax.nn.sigmoid(gate_in))
    load("wo").wait()

    def sum_copy(which, bank, n):
        src = R.sum_src
        source = (
            src.at[bank, far_ten, 0],
            src.at[bank, far_ten, 1],
            src.at[bank, near_ten, 0],
            src.at[bank, over_ten, 1],
            R.sum_via.at[bank, 0],
            R.sum_via.at[bank, 1],
        )[n]
        peer = (near_ten, over_ten, near_ten, over_ten, over_ten, near_ten)[n]
        return remote(
            source,
            R.sum_slots.at[bank, n],
            R.sum_sem.at[which, 0, n],
            R.sum_sem.at[which, 1, n],
            "tensor",
            peer,
        )

    def sum_start(which, bank, value=None):
        if value is not None:
            R.sum_src[bank] = value.reshape(n_ten, 2, own_rows // 2, model)
        for n in range(4):
            sum_copy(which, bank, n).start()

    def sum_relay(which, bank):
        sum_copy(which, bank, 0).wait_recv()
        R.sum_via[bank, 0] = R.sum_slots[bank, 0] + R.sum_src[bank, over_ten, 0]
        sum_copy(which, bank, 4).start()
        sum_copy(which, bank, 1).wait_recv()
        R.sum_via[bank, 1] = R.sum_slots[bank, 1] + R.sum_src[bank, near_ten, 1]
        sum_copy(which, bank, 5).start()

    def sum_end(which, bank):
        for n in range(2, 6):
            sum_copy(which, bank, n).wait_recv()
        slots = R.sum_slots
        own = R.sum_src
        return jnp.concatenate(
            [
                own[bank, ten, 0] + slots[bank, 2] + slots[bank, 4],
                own[bank, ten, 1] + slots[bank, 3] + slots[bank, 5],
            ],
            axis=0,
        )

    def sum_sent(which, bank):
        for n in range(6):
            sum_copy(which, bank, n).wait_send()

    def share_copy(which, n, arriving=False):
        if arriving:
            owner = (near_ten, over_ten, near_ten, over_ten, far_ten, far_ten)[n]
        else:
            owner = (ten, ten, ten, ten, near_ten, over_ten)[n]
        spot = R.shared.at[min(which, 3), owner, (0, 1, 1, 0, 0, 1)[n]]
        return remote(
            spot,
            spot,
            R.share_sem.at[which, 0, n],
            R.share_sem.at[which, 1, n],
            "tensor",
            (near_ten, over_ten, near_ten, over_ten, over_ten, near_ten)[n],
        )

    def share_start(which, value=None):
        if value is not None:
            R.shared[which, ten] = value.reshape(2, own_rows // 2, model)
        for n in range(4):
            share_copy(which, n).start()

    def share_relay(which):
        share_copy(which, 0, True).wait_recv()
        share_copy(which, 4).start()
        share_copy(which, 1, True).wait_recv()
        share_copy(which, 5).start()

    def share_end(which):
        for n in range(2, 6):
            share_copy(which, n, True).wait_recv()

    def share_sent(which):
        for n in range(6):
            share_copy(which, n).wait_send()

    arrays = len(pieces)
    cut = (1, 1, 0, 0, 0)
    heights = [R.made(i).shape[1] for i in range(arrays)]

    def rows(i, piece):
        height = heights[i] // pieces[i]
        return pl.ds(piece * height, height)

    def near_copy(i, step, dest, piece):
        peer = lax.rem(ctx + step, n_ctx)
        return remote(
            R.made(i).at[peer * n_dp + dest, rows(i, piece)],
            R.near(i).at[step - 1, dest, rows(i, piece)],
            R.near_sem(i).at[0, step - 1, dest, piece],
            R.near_sem(i).at[1, step - 1, dest, piece],
            "context",
            peer,
        )

    def line_copy(i, way, dest, piece, peer):
        goal = jnp.where(dest == peer, n_dp, dest) if way == 1 else dest
        return remote(
            R.line(i).at[dest, rows(i, piece)],
            R.line(i).at[goal, rows(i, piece)],
            R.line_sem(i).at[0, way, dest, piece],
            R.line_sem(i).at[1, way, dest, piece],
            "dp",
            peer,
        )

    def loop(low, high, body):
        if high - low == 1:
            body(low)
        else:

            def lap(index, carry):
                body(index)
                return carry

            lax.fori_loop(low, high, lap, 0)

    def over_pieces(i, body):
        loop(0, pieces[i], body)

    def over_steps(body):
        loop(1, n_ctx, body)

    def takes_part(i, dest):
        if not cut[i]:
            return True
        if dest == 0:
            return dp < last
        if dest == last:
            return dp > 0
        return jnp.logical_not(is_end)

    def guarded(condition, body):
        if condition is True:
            body()
        else:
            pl.when(condition)(body)

    def put(i, owner, dest):
        made = R.made(i)
        cols = pl.ds(pl.multiple_of(owner * part, part), part) if wide else None
        if i < 2:
            right = R.mixed if i == 0 else R.gpair
            left = R.g_s if i == 0 else R.n2_s
            both = jnp.logical_or(
                dp == 1 if dest >= 1 else False, dp == last - 1 if dest < last else False
            )

            @pl.when(both)
            def _():
                if wide:
                    made[owner] = mm(right[...], left[:, cols])
                else:
                    made[owner] = mm_nt(R.left(i)[owner], right[...])

            @pl.when(jnp.logical_not(both))
            def _():
                if wide:
                    made[owner] = mm(right[:, :tokens], left[:tokens, cols])
                else:
                    made[owner] = mm_nt(R.left(i)[owner, :, :tokens], right[:, :tokens])

        elif i == 2:
            if wide:
                made[owner] = mm(R.gated[...], R.n2_s[:tokens, cols])
            else:
                made[owner] = mm_nt(R.left0[owner, :, :tokens], R.gated[...])
        elif i == 3:
            made[owner] = mm(R.left3[owner], R.gproj[...])

    def make(i, dest):
        def body():
            def step_body(step):
                put(i, lax.rem(ctx + step, n_ctx) * n_dp + dest, dest)
                over_pieces(i, lambda piece: near_copy(i, step, dest, piece).start())

            over_steps(step_body)
            put(i, ctx * n_dp + dest, dest)

        guarded(takes_part(i, dest), body)

    def own_sum(i, dest, piece):
        total = R.made(i)[ctx * n_dp + dest, rows(i, piece)]
        for step in range(1, n_ctx):
            near_copy(i, step, dest, piece).wait_recv()
            total = total + R.near(i)[step - 1, dest, rows(i, piece)]
        return total

    def first_send(i, way, dest):
        start = cut[i] if way == 0 else last - cut[i]
        if dest <= start if way == 0 else dest >= start:
            return

        @pl.when(dp == start)
        def _():
            def body(piece):
                R.line(i)[dest, rows(i, piece)] = own_sum(i, dest, piece)
                line_copy(i, way, dest, piece, dp + 1 if way == 0 else dp - 1).start()

            over_pieces(i, body)

    def middle_send(i, way, dest, hop):
        reach = dest - cut[i] if way == 0 else last - cut[i] - dest
        if reach < (2 if hop == 1 else 3):
            return
        if way == 0:
            active = dp == cut[i] + 1
            if hop > 1:
                active = jnp.logical_and(dp > cut[i] + 1, dp < dest)
        else:
            active = dp == last - cut[i] - 1
            if hop > 1:
                active = jnp.logical_and(dp < last - cut[i] - 1, dp > dest)
        peer = dp + 1 if way == 0 else dp - 1

        @pl.when(active)
        def _():
            def body(piece):
                own = own_sum(i, dest, piece)
                line_copy(i, way, dest, piece, dp).wait_recv()
                R.line(i)[dest, rows(i, piece)] = (
                    R.line(i)[dest, rows(i, piece)] + own
                )
                line_copy(i, way, dest, piece, peer).start()

            over_pieces(i, body)

    def makes(i, k):
        for dest in dict.fromkeys((last - k, k)):
            make(i, dest)

    def firsts(i, k):
        first_send(i, 0, last - k)
        first_send(i, 1, k)

    def middles(i, k, hop):
        middle_send(i, 0, last - k, hop)
        middle_send(i, 1, k, hop)

    laps = -(-n_dp // 2)

    def build(i, begin=0):
        for k in range(begin, laps):
            makes(i, k)
            firsts(i, k)
        for k in range(laps, last):
            firsts(i, k)

    def finish(i, out):
        def body(piece):
            span = rows(i, piece)
            here = ctx * n_dp + dp
            made = R.made(i)
            made[here, span] = own_sum(i, dp, piece)

            @pl.when(dp > cut[i])
            def _():
                line_copy(i, 0, dp, piece, dp).wait_recv()
                made[here, span] += R.line(i)[dp, span]

            @pl.when(dp < last - cut[i])
            def _():
                line_copy(i, 1, dp, piece, dp).wait_recv()
                made[here, span] += R.line(i)[n_dp, span]

            out(span, made[here, span])

        over_pieces(i, body)

    def drain(i):
        for dest in range(n_dp):

            def near_sent(dest=dest):
                def body(piece):
                    for step in range(1, n_ctx):
                        near_copy(i, step, dest, piece).wait_send()

                over_pieces(i, body)

            guarded(takes_part(i, dest), near_sent)
            if dest > cut[i]:

                @pl.when(jnp.logical_and(dp >= cut[i], dp < dest))
                def _(dest=dest):
                    over_pieces(
                        i, lambda piece: line_copy(i, 0, dest, piece, dp + 1).wait_send()
                    )

            if dest < last - cut[i]:

                @pl.when(jnp.logical_and(dp <= last - cut[i], dp > dest))
                def _(dest=dest):
                    over_pieces(
                        i, lambda piece: line_copy(i, 1, dest, piece, dp - 1).wait_send()
                    )

    def turned(value):
        return value.T.reshape(owners, part, value.shape[0]).astype(bf16)

    sum_start(0, 0, mm(gated.astype(bf16), R.wo_s[...]))
    R.gated[...] = gated.T.astype(bf16)
    sum_relay(0, 0)
    R.left3[...] = turned(norm_one()[1].astype(f32))
    hid = R.x_s[mine, :].astype(f32) + sum_end(0, 0)
    R.hid[...] = hid
    gain2 = R.gain2[...]
    share_start(0, (hid * rms_scale(hid) * gain2).astype(bf16).astype(f32))

    @pl.when(is_end)
    def _():
        ext_copy(1, end_peer).start()

    load("wg").wait()
    load("wu").wait()
    load("wd").wait()
    sum_sent(0, 0)
    share_relay(0)
    R.gm[...] = mm_nt(R.wd_s[...], R.g_s[:tokens, :])

    @pl.when(absorbs)
    def _():
        ext_copy(0, absorb_peer).wait_recv()
        R.g_s[tokens:, :] = R.shared[2].reshape(tokens, model).astype(bf16)
        ext_copy(1, absorb_peer).wait_recv()
        share_start(4)

    share_end(0)

    def feed_forward(half):
        span = slice(half * tokens, (half + 1) * tokens)
        n2 = R.n2_s[span, :]
        ffn_gate = mm_nt(R.wgu[:hidden, :], n2)
        ffn_up = mm_nt(R.wgu[hidden:, :], n2)
        R.mixed[:, span] = (ffn_gate * jax.nn.sigmoid(ffn_gate) * ffn_up).astype(bf16)
        R.ffn_gate[...] = ffn_gate
        R.ffn_up[...] = ffn_up

    def feed_back(half):
        span = slice(half * tokens, (half + 1) * tokens)
        grad_mixed, ffn_gate, ffn_up = R.gm[...], R.ffn_gate[...], R.ffn_up[...]
        sig = jax.nn.sigmoid(ffn_gate)
        R.gpair[:hidden, span] = (
            grad_mixed * ffn_up * (sig * (1.0 + ffn_gate * (1.0 - sig)))
        ).astype(bf16)
        R.gpair[hidden:, span] = (grad_mixed * (ffn_gate * sig)).astype(bf16)

    R.n2_s[:tokens, :] = R.shared[0].reshape(tokens, model).astype(bf16)
    feed_forward(0)
    feed_back(0)

    @pl.when(absorbs)
    def _():
        share_relay(4)
        R.gm[...] = mm_nt(R.wd_s[...], R.g_s[tokens:, :])

    ffn_part = mm_tn(R.gpair[:, :tokens], R.wgu[...])
    R.sum_src[0] = ffn_part.reshape(R.sum_src.shape[1:])

    @pl.when(absorbs)
    def _():
        share_end(4)

    sum_start(1, 0)

    @pl.when(absorbs)
    def _():
        R.n2_s[tokens:, :] = R.shared[3].reshape(tokens, model).astype(bf16)
        feed_forward(1)

    if not wide:
        for at in range(0, 2 * tokens, 128):
            span = slice(at, at + 128)
            R.left0[:, :, span] = turned(R.g_s[span, :].astype(f32))
            R.left1[:, :, span] = turned(R.n2_s[span, :].astype(f32))
    makes(0, 0)
    sum_relay(1, 0)
    firsts(0, 0)

    @pl.when(absorbs)
    def _():
        feed_back(1)

    grad_normed_two = sum_end(1, 0)
    hid = R.hid[...]
    grad_two_rows, gain_two_part = norm_back(hid, rms_scale(hid), gain2, grad_normed_two)
    grad_hidden = R.g_s[mine, :].astype(f32) + grad_two_rows
    R.gh[...] = grad_hidden
    share_start(1, grad_hidden.astype(bf16).astype(f32))
    sum_sent(1, 0)
    build(0, 1)
    share_relay(1)

    @pl.when(is_end)
    def _():
        ext_copy(0, end_peer).wait_send()

    sum_start(2, 1, mm_tn(R.mixed[:, :tokens], R.wd_s[...]))
    build(1)
    middles(0, 0, 1)
    share_end(1)

    R.n2_s[:tokens, :] = R.shared[1].reshape(tokens, model).astype(bf16)
    grad_gated = mm_nt(R.n2_s[:tokens, :], R.wo_s[...])
    o = R.o_s[...]
    gate_in = R.proj[:, 2 * key_dim + value_dim :]
    scale_h = lax.rsqrt(jnp.mean(o * o, axis=-1, keepdims=True) + EPS_HEAD)
    sig = jax.nn.sigmoid(gate_in)
    soft = gate_in * sig
    hgain = R.hgain[...]
    normal = o * scale_h
    head_part = jnp.sum(grad_gated * normal * soft, axis=0, keepdims=True)
    R.gproj[:, 2 * key_dim + value_dim :] = (
        grad_gated * normal * hgain * (sig * (1.0 + gate_in * (1.0 - sig)))
    ).astype(bf16)
    back = grad_gated * hgain * soft
    go = scale_h * (
        back - normal * scale_h * jnp.mean(back * o, axis=-1, keepdims=True)
    )
    R.go[...] = go
    R.pair_back[:, :value_dim] = hdot(R.decayed[...], go, ((0,), (0,)))
    R.pair_back[:, value_dim:] = R.pair[:, value_dim:]
    for step in range(1, n_ctx):
        ctx_copy(1, R.pair_back, R.back_slots, step).start()
    sum_relay(2, 1)
    if not wide:
        R.left0[:, :, :tokens] = turned(R.shared[1].reshape(tokens, model))
    build(2)
    for step in range(1, n_ctx):
        ctx_copy(1, R.pair_back, R.back_slots, step).wait_recv()
    fold(R.later, R.back_slots, True)
    gla_backward(
        R.proj, R.cumuls, R.states, R.entry, R.later, R.go, R.gproj, R.dr
    )
    grad_logits = R.dr[...] * jax.nn.sigmoid(-R.logits[...]) / GATE_NORM
    grad_low = hdot(grad_logits, R.wlu[...].astype(f32), ((1,), (1,)))

    @pl.when(absorbs)
    def _():
        share_sent(4)

    sum_start(
        3,
        0,
        mm_nt(R.gproj[...], R.wcat[...])
        + hdot(grad_low, R.wld[...].astype(f32), ((1,), (0,))),
    )
    scaled, n1f = norm_one()
    low_down = hdot(grad_low, n1f.astype(f32), ((0,), (0,)))
    low_up = hdot(R.low[...], grad_logits, ((0,), (0,)))
    bias_part = jnp.sum(grad_logits, axis=0, keepdims=True)
    gain_one_part = jnp.sum(
        R.sum_src[0].reshape(tokens, model) * scaled, axis=0, keepdims=True
    )
    R.made4[...] = jnp.zeros_like(R.made4)
    part_head = value_dim // owners
    part_key = key_dim // owners
    tail = R.tail_slots.shape[1]
    for owner in range(owners):
        span = slice(owner * part, (owner + 1) * part)
        R.made4[owner, :rank, :part] = low_down[:, span]
        R.made4[owner, rank : rank + 1, :part] = gain_one_part[:, span]
        R.made4[owner, rank + 1 : rank + 2, :part] = gain_two_part[:, span]
        R.made4[owner, rank + 2 : rank + 3, :part_head] = head_part[
            :, owner * part_head : (owner + 1) * part_head
        ]
        span = slice(owner * part_key, (owner + 1) * part_key)
        R.made4[owner, tail : tail + rank, :part_key] = low_up[:, span]
        R.made4[owner, tail + rank : tail + rank + 1, :part_key] = bias_part[:, span]
    build(4)
    build(3)
    sum_relay(3, 0)
    for k in range(last):
        middles(2, k, 1)
    for k in range(last):
        middles(4, k, 1)
    middles(1, 0, 1)
    result = R.hid[...] + sum_end(2, 1)
    share_start(2, result.astype(bf16).astype(f32))
    middles(3, 0, 1)
    grad_normed_one = sum_end(3, 0)
    own_in = R.x_s[mine, :].astype(f32)
    grad_one_rows, _ = norm_back(own_in, rms_scale(own_in), R.gain1[...], grad_normed_one)
    share_relay(2)
    share_start(3, R.gh[...] + grad_one_rows)
    for i in range(2):
        for k in range(1, last):
            middles(i, k, 1)
    for k in range(1, last):
        middles(3, k, 1)
    share_relay(3)
    for i in (0, 1, 2, 4, 3):
        for k in range(last):
            middles(i, k, 2)

    def into(name):
        def out(span, value):
            getattr(R, name)[span, :] = value

        return out

    def put_proj(span, value):
        R.gq[span, :] = value[:, :key_dim]
        R.gk[span, :] = value[:, key_dim : 2 * key_dim]
        R.gv[span, :] = value[:, 2 * key_dim : 2 * key_dim + value_dim]
        R.ggo[span, :] = value[:, 2 * key_dim + value_dim :]

    def leave(name):
        return pltpu.make_async_copy(
            getattr(R, name), getattr(R, "out_" + name), R.leave_sem.at[LEAVES.index(name)]
        )

    finish(0, into("gdown"))
    leave("gdown").start()
    finish(1, into("gpairs"))
    leave("gpairs").start()
    share_end(2)
    R.result[...] = R.shared[2].reshape(tokens, model).astype(bf16)
    leave("result").start()
    share_end(3)
    R.gin[...] = R.shared[3].reshape(tokens, model)
    leave("gin").start()
    finish(2, into("gout"))
    leave("gout").start()
    finish(4, into("pack"))
    R.tail_slots[ten] = R.pack[:tail, :]

    def tail_copy(sender, peer, step):
        spot = R.tail_slots.at[sender]
        return remote(
            spot, spot, R.tail_sem.at[0, step - 1], R.tail_sem.at[1, step - 1], "tensor", peer
        )

    for step in range(1, n_ten):
        tail_copy(ten, lax.rem(ten + step, n_ten), step).start()
    finish(3, put_proj)
    for name in ("gq", "gk", "gv", "ggo"):
        leave(name).start()
    for step in range(1, n_ten):
        sender = lax.rem(ten + n_ten - step, n_ten)
        tail_copy(sender, sender, step).wait_recv()
    total = R.tail_slots[0]
    for index in range(1, n_ten):
        total = total + R.tail_slots[index]
    R.pack[:tail, :] = total
    leave("pack").start()

    for step in range(1, n_ctx):
        ctx_copy(0, R.pair, R.pair_slots, step).wait_send()
        ctx_copy(1, R.pair_back, R.back_slots, step).wait_send()
    sum_sent(2, 1)
    sum_sent(3, 0)
    for which in range(4):
        share_sent(which)

    @pl.when(is_end)
    def _():
        ext_copy(1, end_peer).wait_send()

    for i in range(arrays):
        drain(i)
    for step in range(1, n_ten):
        tail_copy(ten, lax.rem(ten + step, n_ten), step).wait_send()
    for name in LEAVES:
        leave(name).wait()


def hand_out_kernel(moves, n_in, n_big, *refs):
    ins, pack_ref = refs[: n_in - 1], refs[n_in - 1]
    big = refs[n_in : n_in + n_big]
    small = refs[n_in + n_big : n_in + n_big + 6]
    held = refs[n_in + n_big + 6 : -1]
    sems = refs[-1]

    def arrive(at):
        return pltpu.make_async_copy(ins[at], held[at], sems.at[0, at])

    def depart(at):
        source, first, rows = moves[at]
        src = held[source] if rows is None else held[source].at[first : first + rows]
        return pltpu.make_async_copy(src, big[at], sems.at[1, at])

    for at in range(len(ins)):
        arrive(at).start()
    for at in range(len(ins)):
        arrive(at).wait()
        for move in range(n_big):
            if moves[move][0] == at:
                depart(move).start()
    low_down, gain1, gain2, hgain, low_up, bias = small
    rank, part = low_down.shape
    tail = -(-(rank + 3) // 8) * 8
    low_down[...] = pack_ref[:rank, :part]
    gain1[...] = pack_ref[rank : rank + 1, :part]
    gain2[...] = pack_ref[rank + 1 : rank + 2, :part]
    hgain[...] = pack_ref[rank + 2 : rank + 3, : hgain.shape[1]]
    low_up[...] = pack_ref[tail : tail + rank, : low_up.shape[1]]
    bias[...] = pack_ref[tail + rank : tail + rank + 1, : bias.shape[1]]
    for at in range(n_big):
        depart(at).wait()


def shards(
    inputs,
    norm_gain1,
    w_query,
    w_key,
    w_value,
    w_gate_out,
    w_low_down,
    w_low_up,
    forget_bias,
    head_gain,
    w_output,
    norm_gain2,
    w_ffn_gate,
    w_ffn_up,
    w_ffn_down,
    cotangent,
):
    bf16, f32 = jnp.bfloat16, jnp.float32
    n_ctx, n_dp, n_ten = (lax.axis_size(axis) for axis in ("context", "dp", "tensor"))
    owners = n_ctx * n_dp
    model = inputs.shape[-1]
    x = inputs.reshape(-1, model)
    tokens = x.shape[0]
    key_dim, value_dim, hidden = w_query.shape[1], w_value.shape[1], w_ffn_gate.shape[1]
    assert inputs.shape[0] == 1 and head_gain.shape[0] == value_dim
    assert n_ten == 4 and n_dp >= 4
    rank = w_low_down.shape[1]
    part = model // owners
    wide = part % 128 == 0
    own_rows = tokens // n_ten
    width = 2 * key_dim + 2 * value_dim
    tail = -(-(rank + 3) // 8) * 8
    pack_rows = tail + -(-(rank + 1) // 8) * 8

    ins = dict(
        x=x,
        gain1=norm_gain1[None],
        wq=w_query,
        wk=w_key,
        wv=w_value,
        wgo=w_gate_out,
        wld=w_low_down.T,
        wlu=w_low_up,
        bias=forget_bias[None],
        hgain=head_gain[None],
        wo=w_output,
        gain2=norm_gain2[None],
        wg=w_ffn_gate.T,
        wu=w_ffn_up.T,
        wd=w_ffn_down,
        g=cotangent.reshape(-1, model),
    )

    def owned(extent):
        return (extent, part) if wide else (part, extent)

    shapes = [owned(hidden), owned(2 * hidden), owned(value_dim), (part, width), (pack_rows, 128)]
    outs = dict(
        result=((tokens, model), bf16),
        gin=((tokens, model), f32),
        gq=((part, key_dim), f32),
        gk=((part, key_dim), f32),
        gv=((part, value_dim), f32),
        ggo=((part, value_dim), f32),
        gout=(shapes[2], f32),
        gpairs=(shapes[1], f32),
        gdown=(shapes[0], f32),
        pack=((pack_rows, 128), f32),
    )
    pieces = []
    for shape in shapes:
        count = 2
        while shape[0] % (count * 8):
            count //= 2
        pieces.append(count if shape[0] * shape[1] > 16384 else 1)

    dma = pltpu.SemaphoreType.DMA
    scratch = dict(
        x_s=pltpu.VMEM((tokens, model), bf16),
        g_s=pltpu.VMEM((2 * tokens, model), bf16),
        ext_sem=dma((2, 2)),
        wcat=pltpu.VMEM((model, width), bf16),
        wo_s=pltpu.VMEM((value_dim, model), bf16),
        wgu=pltpu.VMEM((2 * hidden, model), bf16),
        wd_s=pltpu.VMEM((hidden, model), bf16),
        load_sem=dma((len(LOADS),)),
        leave_sem=dma((len(LEAVES),)),
        n2_s=pltpu.VMEM((2 * tokens, model), bf16),
        proj=pltpu.VMEM((tokens, width), f32),
        low=pltpu.VMEM((tokens, rank), f32),
        logits=pltpu.VMEM((tokens, key_dim), f32),
        rates=pltpu.VMEM((tokens, key_dim), f32),
        cumuls=pltpu.VMEM((tokens, key_dim), f32),
        o_s=pltpu.VMEM((tokens, value_dim), f32),
        decayed=pltpu.VMEM((tokens, key_dim), f32),
        states=pltpu.VMEM((tokens // BLOCK, key_dim, value_dim), f32),
        pair=pltpu.VMEM((key_dim, value_dim + key_dim), f32),
        pair_back=pltpu.VMEM((key_dim, value_dim + key_dim), f32),
        pair_slots=pltpu.VMEM((n_ctx - 1, key_dim, value_dim + key_dim), f32),
        back_slots=pltpu.VMEM((n_ctx - 1, key_dim, value_dim + key_dim), f32),
        ctx_sem=dma((2, 2, n_ctx - 1)),
        entry=pltpu.VMEM((key_dim, value_dim), f32),
        later=pltpu.VMEM((key_dim, value_dim), f32),
        gm=pltpu.VMEM((hidden, tokens), f32),
        ffn_gate=pltpu.VMEM((hidden, tokens), f32),
        ffn_up=pltpu.VMEM((hidden, tokens), f32),
        gated=pltpu.VMEM((value_dim, tokens), bf16),
        sum_src=pltpu.VMEM((2, n_ten, 2, own_rows // 2, model), f32),
        sum_slots=pltpu.VMEM((2, 6, own_rows // 2, model), f32),
        sum_via=pltpu.VMEM((2, 2, own_rows // 2, model), f32),
        sum_sem=dma((4, 2, 6)),
        shared=pltpu.VMEM((4, n_ten, 2, own_rows // 2, model), f32),
        share_sem=dma((5, 2, 6)),
        hid=pltpu.VMEM((own_rows, model), f32),
        gh=pltpu.VMEM((own_rows, model), f32),
        mixed=pltpu.VMEM((hidden, 2 * tokens), bf16),
        gpair=pltpu.VMEM((2 * hidden, 2 * tokens), bf16),
        go=pltpu.VMEM((tokens, value_dim), f32),
        dr=pltpu.VMEM((tokens, key_dim), f32),
        gproj=pltpu.VMEM((tokens, width), bf16),
        tail_slots=pltpu.VMEM((n_ten, tail, 128), f32),
        tail_sem=dma((2, n_ten - 1)),
        left3=pltpu.VMEM((owners, part, tokens), bf16),
    )
    if not wide:
        scratch["left0"] = pltpu.VMEM((owners, part, 2 * tokens), bf16)
        scratch["left1"] = pltpu.VMEM((owners, part, 2 * tokens), bf16)
    for i, shape in enumerate(shapes):
        scratch["made%d" % i] = pltpu.VMEM((owners,) + shape, f32)
        scratch["near%d" % i] = pltpu.VMEM((n_ctx - 1, n_dp) + shape, f32)
        scratch["line%d" % i] = pltpu.VMEM((n_dp + 1,) + shape, f32)
        scratch["near_sem%d" % i] = dma((2, n_ctx - 1, n_dp, pieces[i]))
        scratch["line_sem%d" % i] = dma((2, 2, n_dp, pieces[i]))

    for name in LEAVES:
        scratch[name] = pltpu.VMEM(*outs[name])
    names = tuple(ins) + tuple("out_" + name for name in outs) + tuple(scratch)
    made = pl.pallas_call(
        functools.partial(block_kernel, (n_ctx, n_dp, n_ten), names, tuple(pieces), wide),
        out_shape=tuple(jax.ShapeDtypeStruct(shape, kind) for shape, kind in outs.values()),
        in_specs=[
            pl.BlockSpec(memory_space=pl.ANY if name in LOADS else VMEM) for name in ins
        ],
        out_specs=tuple([pl.BlockSpec(memory_space=pl.ANY)] * len(outs)),
        scratch_shapes=list(scratch.values()),
        compiler_params=pltpu.CompilerParams(
            collective_id=0, has_side_effects=True, vmem_limit_bytes=VMEM_LIMIT
        ),
        name="gla_block",
    )(*ins.values())
    part_head = value_dim // owners
    part_key = key_dim // owners
    moves, big_shapes = [], []
    for at, name in enumerate(list(outs)[:-1]):
        shape, kind = outs[name]
        if name == "gpairs" and wide:
            for half in range(2):
                moves.append((at, half * hidden, hidden))
                big_shapes.append(((hidden, part), kind))
        else:
            moves.append((at, 0, None))
            big_shapes.append((shape, kind))
    small_shapes = [
        (rank, part),
        (1, part),
        (1, part),
        (1, part_head),
        (rank, part_key),
        (1, part_key),
    ]
    done = pl.pallas_call(
        functools.partial(hand_out_kernel, tuple(moves), len(made), len(moves)),
        out_shape=tuple(
            [jax.ShapeDtypeStruct(shape, kind) for shape, kind in big_shapes]
            + [jax.ShapeDtypeStruct(shape, f32) for shape in small_shapes]
        ),
        in_specs=[pl.BlockSpec(memory_space=pl.ANY)] * (len(made) - 1)
        + [pl.BlockSpec(memory_space=VMEM)],
        out_specs=tuple(
            [pl.BlockSpec(memory_space=pl.ANY)] * len(moves)
            + [pl.BlockSpec(memory_space=VMEM)] * len(small_shapes)
        ),
        scratch_shapes=[pltpu.VMEM(shape, kind) for shape, kind in list(outs.values())[:-1]]
        + [dma((2, len(moves)))],
        name="hand_out",
    )(*made)
    low_down, gain1, gain2, hgain, low_up, bias = done[len(moves) :]
    result, gin, gq, gk, gv, ggo, gout = done[:7]
    if wide:
        ggate, gup, gdown = done[7].T, done[8].T, done[9]
    else:
        ggate, gup = done[7][:, :hidden], done[7][:, hidden:]
        gdown, gout = done[8].T, gout.T
    return (
        result.reshape(inputs.shape),
        gin.reshape(inputs.shape),
        gain1.reshape(-1),
        gq,
        gk,
        gv,
        ggo,
        low_down.T,
        low_up,
        bias.reshape(-1),
        hgain.reshape(-1),
        gout,
        gain2.reshape(-1),
        ggate,
        gup,
        gdown,
    )


def solution(mesh):
    return jax.shard_map(
        shards,
        mesh=mesh,
        in_specs=(
            P("dp", "context", None),
            P(),
            P(None, "tensor"),
            P(None, "tensor"),
            P(None, "tensor"),
            P(None, "tensor"),
            P(),
            P(None, "tensor"),
            P("tensor"),
            P(),
            P("tensor", None),
            P(),
            P(None, "tensor"),
            P(None, "tensor"),
            P("tensor", None),
            P("dp", "context", None),
        ),
        out_specs=(
            P("dp", "context", None),
            P("dp", "context", None),
            P(("context", "dp")),
            P(("context", "dp"), "tensor"),
            P(("context", "dp"), "tensor"),
            P(("context", "dp"), "tensor"),
            P(("context", "dp"), "tensor"),
            P(("context", "dp"), None),
            P(None, ("tensor", "context", "dp")),
            P(("tensor", "context", "dp")),
            P(("context", "dp")),
            P("tensor", ("context", "dp")),
            P(("context", "dp")),
            P(("context", "dp"), "tensor"),
            P(("context", "dp"), "tensor"),
            P("tensor", ("context", "dp")),
        ),
        check_vma=False,
    )
```
